32 devices in a mesh: grp: 2 (over x), col: 16 (over z, y, core).
Axes of the slice: x: 2, y: 2, z: 4, core: 2. Of those that a mesh axis runs over, the one named last changes fastest.
Arguments:
- database: int32 [256, 4096], P('col', 'grp'), parts along dimension 1, may hold values from 0 to 255
- queries: int32 [16, 256], P('grp', 'col'), parts along dimension 0, may hold values from -2147483648 to 2147483646
- key_rows: int32 [16, 8192], P('grp', 'col'), parts along dimension 0, may hold values from -2147483648 to 2147483646
- hint: int32 [4, 1024], P('grp'), parts along dimension 0, may hold values from -2147483648 to 2147483646
- assignment: int32 [32], P('grp'), parts along dimension 0, may hold values from 0 to 15, each once
Outputs:
- packed: float32 [32, 2, 1024], P(('grp', 'col')), parts along dimension 0
The draws below stay inside these ranges and needn't reach their ends.
There are 2 independent parts, one for each index of `grp`. The reference program is written for one: setup_inputs(seed, part) draws one part's arguments, and reference() takes and returns one part's arrays. A program takes and returns all parts, laid end to end along the dimension named above; each array names one. Nothing has to cross between parts.
Inputs may be any that keep to these rules, and one draw needn't show every extreme that they name: `assignment`: every unit appears in exactly one slot.
All inputs are finite; a program needn't handle non-finite values.
Results may differ from the reference program's by a relative error of at most 0.0003.
Values sent between devices are 32-bit elements; how exact they have to be, the bound alone decides.
A program may use at most 128 MiB of HBM per device.

```python
import jax
import jax.numpy as jnp
from jax import lax

CYCLE = 1024
LEVELS = 2
DIGITS = 2
CLIENTS = 8
POLYS = 2
ROWS = 2048
COLS = 256
UNITS = 16
KEY_LEN = 8192


def plant(result, key, least, top_value):
    longest = result.shape.index(max(result.shape))
    spots = []
    for shift in (0, 1):
        where = [jax.random.randint(jax.random.fold_in(key, axis), (), 0, length) for axis, length in enumerate(result.shape)]
        where[longest] = (where[longest] + shift) % result.shape[longest]
        spots.append(tuple(where))
    return result.at[spots[0]].set(least).at[spots[1]].set(top_value)


def setup_inputs(seed: int = 0, part: int = 0) -> dict:
    seeds = jax.random.split(jax.random.key(seed), 6)
    part_keys = jax.random.split(jax.random.fold_in(seeds[5], part), 6)
    database = plant(jax.random.randint(part_keys[0], (COLS, ROWS), 0, 256), jax.random.fold_in(part_keys[0], 1), 0, 255).astype(jnp.int32)
    queries = plant(jax.random.randint(part_keys[1], (CLIENTS, COLS), -2147483648, 2147483647), jax.random.fold_in(part_keys[1], 1), -2147483648, 2147483646).astype(jnp.int32)
    key_rows = plant(jax.random.randint(part_keys[2], (CLIENTS, KEY_LEN), -2147483648, 2147483647), jax.random.fold_in(part_keys[2], 1), -2147483648, 2147483646).astype(jnp.int32)
    hint = plant(jax.random.randint(part_keys[3], (POLYS, CYCLE), -2147483648, 2147483647), jax.random.fold_in(part_keys[3], 1), -2147483648, 2147483646).astype(jnp.int32)
    assignment = jax.random.permutation(part_keys[4], UNITS).astype(jnp.int32)
    return {"database": database, "queries": queries, "key_rows": key_rows, "hint": hint, "assignment": assignment}


def automorph(polynomial, galois):
    cycle_width = polynomial.shape[0]
    inverse = pow(galois, -1, 2 * cycle_width)
    source = (jnp.arange(cycle_width, dtype=jnp.int32) * inverse) % (2 * cycle_width)
    picked = jnp.take(polynomial, source % cycle_width, axis=0)
    return jnp.where(source < cycle_width, picked, -picked)


def toeplitz(key_poly):
    cycle_width = key_poly.shape[0]
    shifted = jnp.concatenate([-key_poly[1:], key_poly, -key_poly[:1]])
    tiled_rows = jnp.tile(shifted, cycle_width)[: cycle_width * (2 * cycle_width - 1)]
    return tiled_rows.reshape(cycle_width, 2 * cycle_width - 1)[:, cycle_width - 1:2 * cycle_width - 1]


def switch_section(mask_poly, value_poly, section_keys, galois):
    cycle_width = mask_poly.shape[0]
    rotated_mask = automorph(mask_poly, galois)
    rotated_value = automorph(value_poly, galois)
    switched = jnp.zeros((2 * cycle_width,), jnp.int32)
    for digit_index in range(section_keys.shape[0]):
        digit_row = jnp.bitwise_and(jnp.right_shift(rotated_mask, 16 * digit_index), 65535)
        matrix = jnp.concatenate([toeplitz(section_keys[digit_index, 0]), toeplitz(section_keys[digit_index, 1])], axis=1)
        switched = switched + jnp.dot(digit_row[None, :], matrix, preferred_element_type=jnp.int32)[0]
    return mask_poly + switched[:cycle_width], value_poly + rotated_value + switched[cycle_width:]


def pack_unit(mask_poly, value_poly, key_row):
    cycle_width = mask_poly.shape[0]
    section_table = key_row.reshape(LEVELS, DIGITS, 2, cycle_width)
    for section_index in range(LEVELS):
        galois = cycle_width // (2 ** section_index) + 1
        mask_poly, value_poly = switch_section(mask_poly, value_poly, section_table[section_index], galois)
    return jnp.stack([mask_poly, value_poly])


def reference(database, queries, key_rows, hint, assignment):
    answers = jnp.dot(queries, database, preferred_element_type=jnp.int32)
    unit_rows = answers.reshape(CLIENTS * POLYS, CYCLE)

    def pack_one(unit_index):
        client = unit_index // POLYS
        poly_index = unit_index % POLYS
        mask_poly = lax.dynamic_index_in_dim(hint, poly_index, 0, keepdims=False)
        value_poly = lax.dynamic_index_in_dim(unit_rows, unit_index, 0, keepdims=False)
        key_row = lax.dynamic_index_in_dim(key_rows, client, 0, keepdims=False)
        return pack_unit(mask_poly, value_poly, key_row)

    packed_words = lax.map(pack_one, assignment)
    return packed_words.astype(jnp.float32) * (2.0 ** -32)
```

```python
import functools

import jax
import jax.numpy as jnp
from jax import lax
from jax.experimental import pallas as pl
from jax.experimental.pallas import tpu as pltpu
from jax.sharding import PartitionSpec as P

LEVELS = 2
DIGITS = 2
LANES = 128
WORD_BYTES = 4
DIGIT_BYTES = WORD_BYTES // DIGITS
SPAN = LANES // DIGIT_BYTES


def iota(shape, axis):
    return lax.broadcasted_iota(jnp.int32, shape, axis)


def byte_of(words, index):
    return jnp.bitwise_and(jnp.right_shift(words, 8 * index), 255).astype(jnp.float32)


def shifted(poly, amount):
    rows = poly.shape[0]
    amount = amount % (2 * rows * LANES)
    negate, turn = divmod(amount // LANES, rows)
    moved = poly
    if turn:
        moved = pltpu.roll(poly, turn, 0)
        moved = jnp.where(iota(poly.shape, 0) >= turn, moved, -moved)
    return -moved if negate else moved


def automorph(poly, level):
    step = poly.shape[0] * LANES >> level
    period = 2 << level
    residue = jnp.bitwise_and(iota(poly.shape, 1), period - 1)
    out = poly
    for m in range(1, period):
        out = jnp.where(residue == m, shifted(poly, step * m), out)
    return out


def fill_toeplitz(word_poly, toeplitz):
    rows = word_poly.shape[0]
    block = (SPAN, LANES)
    ahead = iota(block, 1) >= iota(block, 0)

    def turned(q):
        row = jnp.broadcast_to(word_poly[q : q + 1], block)
        return pltpu.roll(row, 0, 1, stride=1, stride_axis=0)

    before = turned(rows - 1)
    for q in range(rows):
        here = turned(q)
        words = jnp.where(ahead, here, before)
        for b in range(WORD_BYTES):
            part = byte_of(words, b)
            if q == 0:
                part = jnp.where(ahead, part, -part)
            toeplitz[b * SPAN : (b + 1) * SPAN, q * LANES : (q + 1) * LANES] = part.astype(
                jnp.bfloat16
            )
        before = here


def key_side(keys):
    owner = iota(keys[0][0].shape, 1) // SPAN
    zero = jnp.zeros(keys[0][0].shape, jnp.float32)
    blocks = []
    for s in range(WORD_BYTES):
        for p in range(2):
            for h in range(DIGIT_BYTES):
                tiles = []
                for t in range(DIGITS):
                    tile = zero
                    for a in range(min(s + 1, DIGIT_BYTES)):
                        part = byte_of(keys[t][p], s - a)
                        if a != h:
                            part = pltpu.roll(part, (a - h) % DIGIT_BYTES * SPAN, 1)
                        tile = jnp.where(owner == a, part, tile)
                    tiles.append(tile)
                blocks.append(jnp.concatenate(tiles, axis=1))
    return jnp.concatenate(blocks, axis=0).astype(jnp.bfloat16)


def switch(toeplitz, key_polys, rows):
    products = jnp.dot(
        key_side(key_polys), toeplitz[...], preferred_element_type=jnp.float32
    ).astype(jnp.int32)
    lane = iota((rows, LANES), 1)
    sums = []
    for p in range(2):
        total = jnp.zeros((rows, LANES), jnp.int32)
        for h in range(DIGIT_BYTES):
            words = None
            for s in range(WORD_BYTES):
                at = ((s * 2 + p) * DIGIT_BYTES + h) * rows
                term = jnp.left_shift(products[at : at + rows], 8 * s)
                words = term if words is None else words + term
            out = words[:, :LANES]
            for q in range(1, rows):
                out = out + shifted(words[:, q * LANES : (q + 1) * LANES], q * LANES)
            if h:
                turn = h * SPAN
                carried = pltpu.roll(shifted(out, LANES), turn, 1)
                out = jnp.where(lane >= turn, pltpu.roll(out, turn, 1), carried)
            total = total + out
        sums.append(total)
    return sums


def kernel(
    n, slots, share, width, assign_hbm, database_hbm, queries_hbm, keys_hbm, hint_hbm, out,
    assign, database, queries, keys, hint, loaded, unit_part, unit_keys, masks,
    ans_send, key_send, ans_recv, key_recv, key_words, toeplitz,
    ready, ans_sent, key_sent, ans_got, key_got,
):
    me = lax.axis_index("col")
    clients, columns = queries.shape
    polys, cycle = hint.shape
    rows = cycle // LANES
    key_rows = key_send.shape[1] // slots
    key_pitch = unit_keys.shape[1]
    unit_key_rows = unit_keys.reshape(clients * polys * key_pitch, LANES)
    unit_part_rows = unit_part.reshape(clients * polys * rows, LANES)
    chunks = 4
    chunk = database.shape[1] // chunks
    size = 2
    planes = n // size
    few = n <= LANES // 8
    level_blocks = n // LEVELS
    chip = lax.div(me, size)
    partner = me + 1 - 2 * lax.rem(me, size)
    height = planes // width
    across = lax.rem(chip, width)
    along = lax.div(chip, width)
    level_held = lax.div(me, level_blocks)

    def each(count, body, start=0):
        lax.fori_loop(start, count, lambda i, c: (body(i), c)[1], 0, unroll=few)
    loads = [
        pltpu.make_async_copy(source, target, loaded.at[i])
        for i, (source, target) in enumerate(
            (
                (keys_hbm, keys),
                (assign_hbm, assign),
                (queries_hbm, queries),
                (database_hbm, database),
                (hint_hbm, hint),
            )
        )
    ]
    for i, load in enumerate(loads):
        if i == 3:
            for j in range(chunks):
                at = pl.ds(j * chunk, chunk)
                pltpu.make_async_copy(database_hbm.at[:, at], database.at[:, at], loaded.at[i]).start()
        else:
            load.start()
    def span(start, stop, body):
        lax.fori_loop(start, stop, lambda i, c: (body(i), c)[1], 0)

    def on_chips(start, stop, column, body):
        def both(i):
            first = (i * width + column) * size
            for core in range(size):
                body(first + core)

        span(start, stop, both)

    barrier = pltpu.get_barrier_semaphore()

    def greet(there):
        pl.semaphore_signal(barrier, inc=1, device_id={"col": there})

    greet(partner)
    for column in range(width):
        on_chips(
            jnp.where(column < across, height, along + jnp.where(column == across, 1, 0)),
            height,
            column,
            greet,
        )
    pl.semaphore_wait(barrier, (along + 1) * (across + 1) * size - 1)

    @pl.when(chip == planes - 1)
    def _():
        def announce(i):
            pl.semaphore_signal(ready, inc=1, device_id={"col": i * size + lax.rem(me, size)})

        span(0, planes - 1, announce)
    loads[0].wait()
    lane_owner = iota((clients, LANES), 1) // (LANES // share)
    for j in range(key_rows):
        tile = keys[:, j * LANES : (j + 1) * LANES]
        if share > 1:
            tile = jnp.where(lane_owner == lax.rem(me, share), tile, 0)
        for p in range(polys):
            unit_key_rows[pl.ds(p * key_pitch + j, clients, stride=polys * key_pitch), :] = tile
    loads[1].wait()

    def stage_keys(owner):
        for k in range(slots):
            key_send[owner, k * key_rows : (k + 1) * key_rows, :] = unit_keys[assign[owner * slots + k]][:key_rows]

    def stage_answers(owner):
        for k in range(slots):
            ans_send[owner, k * rows : (k + 1) * rows, :] = unit_part[assign[owner * slots + k]]
    each(n, stage_keys)

    def send_keys(there):
        pltpu.make_async_remote_copy(
            src_ref=key_send.at[there],
            dst_ref=key_recv.at[me],
            send_sem=key_sent,
            recv_sem=key_got.at[level_held],
            device_id={"col": there},
        ).start()

    def send_answers(there):
        pltpu.make_async_remote_copy(
            src_ref=ans_send.at[there],
            dst_ref=ans_recv.at[me],
            send_sem=ans_sent,
            recv_sem=ans_got,
            device_id={"col": there},
        ).start()

    def to_early(send):
        for column in range(width):
            on_chips(
                0,
                jnp.where(column > across, 0, along + jnp.where(column == across, 0, 1)),
                column,
                send,
            )
        send(partner)

    def to_late(send):
        for column in range(width):
            on_chips(jnp.where(column > across, 0, along + 1), height, column, send)
    to_early(send_keys)
    pltpu.make_async_copy(key_send.at[me], key_recv.at[me], key_got.at[level_held]).start()
    loads[2].wait()
    loads[3].wait()
    query_words = queries[...]
    query_bytes = jnp.concatenate(
        [byte_of(query_words, b) for b in range(WORD_BYTES)], axis=0
    ).astype(jnp.bfloat16)
    products = jnp.dot(
        query_bytes,
        database[...].astype(jnp.float32).astype(jnp.bfloat16),
        preferred_element_type=jnp.float32,
    ).astype(jnp.int32)
    partial = products[:clients]
    for b in range(1, WORD_BYTES):
        partial = partial + jnp.left_shift(products[b * clients : (b + 1) * clients], 8 * b)
    for j in range(polys * rows):
        unit_part_rows[pl.ds(j, clients, stride=polys * rows), :] = partial[:, j * LANES : (j + 1) * LANES]
    each(n, stage_answers)
    to_early(send_answers)
    pltpu.make_async_copy(ans_send.at[me], ans_recv.at[me], ans_got).start()
    loads[4].wait()
    for p in range(polys):
        for q in range(rows):
            masks[p, q : q + 1, :] = hint[p : p + 1, q * LANES : (q + 1) * LANES]

    def first_mask(k):
        return masks[lax.rem(assign[me * slots + k], polys)]

    fill_toeplitz(automorph(first_mask(0), 0), toeplitz)
    @pl.when(chip < planes - 1)
    def _():
        pl.semaphore_wait(ready, 1)
        to_late(send_keys)
        to_late(send_answers)

    def wait_blocks(buffer, semaphore, start, count):
        blocks = buffer.at[pl.ds(start, count)]
        pltpu.make_async_copy(blocks, blocks, semaphore).wait()
    switched = []
    for k in range(slots):
        mask = first_mask(k)
        if k:
            fill_toeplitz(automorph(mask, 0), toeplitz)
        added = []
        for level in range(LEVELS):
            if level:
                fill_toeplitz(automorph(mask, level), toeplitz)
            if k == 0:
                wait_blocks(key_recv, key_got.at[level], level * level_blocks, level_blocks)
            for j in range(level * level_blocks // share, (level + 1) * level_blocks // share):
                block = key_recv[j * share, k * key_rows : (k + 1) * key_rows, :]
                for h in range(1, share):
                    block = block + key_recv[j * share + h, k * key_rows : (k + 1) * key_rows, :]
                key_words[j * key_rows : (j + 1) * key_rows, :] = block

            def key_poly(t, p):
                at = ((level * DIGITS + t) * 2 + p) * rows
                return key_words[at : at + rows, :]

            to_mask, to_value = switch(
                toeplitz, [[key_poly(t, p) for p in range(2)] for t in range(DIGITS)], rows
            )
            mask = mask + to_mask
            added.append(to_value)
        switched.append((mask, added))
    wait_blocks(ans_recv, ans_got, 0, n)
    for k, (mask, added) in enumerate(switched):
        value = ans_recv[0, k * rows : (k + 1) * rows, :]
        for j in range(1, n):
            value = value + ans_recv[j, k * rows : (k + 1) * rows, :]
        for level in range(LEVELS):
            value = value + automorph(value, level) + added[level]
        for index, words in enumerate((mask, value)):
            scaled = words.astype(jnp.float32) * 2.0 ** (-32)
            for q in range(rows):
                out[k, index : index + 1, q * LANES : (q + 1) * LANES] = scaled[q : q + 1]
    wait_blocks(key_send, key_sent, 0, n - 1)
    wait_blocks(ans_send, ans_sent, 0, n - 1)


def solution(mesh):
    n = mesh.shape["col"]
    across = 2

    def on_device(database, queries, key_rows, hint, assignment):
        clients = queries.shape[0]
        polys, cycle = hint.shape
        rows = cycle // LANES
        slots = assignment.shape[0] // n
        width = key_rows.shape[1]
        share = max(1, LANES // width)
        if share > 1:
            key_rows = jnp.tile(key_rows, (1, share))
        tiles = key_rows.shape[1] // LANES
        place = pl.BlockSpec(memory_space=pltpu.HBM)
        return pl.pallas_call(
            functools.partial(kernel, n, slots, share, across),
            out_shape=pltpu.VMEM((slots, 2, cycle), jnp.float32),
            in_specs=[place] * 5,
            out_specs=pl.BlockSpec(memory_space=pltpu.VMEM),
            scratch_shapes=[
                pltpu.SMEM(assignment.shape, jnp.int32),
                pltpu.VMEM(database.shape, jnp.int32),
                pltpu.VMEM(queries.shape, jnp.int32),
                pltpu.VMEM(key_rows.shape, jnp.int32),
                pltpu.VMEM(hint.shape, jnp.int32),
                pltpu.SemaphoreType.DMA((5,)),
                pltpu.VMEM((polys * clients, rows, LANES), jnp.int32),
                pltpu.VMEM((polys * clients, -(-tiles // 8) * 8, LANES), jnp.int32),
                pltpu.VMEM((polys, rows, LANES), jnp.int32),
                pltpu.VMEM((n, slots * rows, LANES), jnp.int32),
                pltpu.VMEM((n, slots * tiles, LANES), jnp.int32),
                pltpu.VMEM((n, slots * rows, LANES), jnp.int32),
                pltpu.VMEM((n, slots * tiles, LANES), jnp.int32),
                pltpu.VMEM((n // share * tiles, LANES), jnp.int32),
                pltpu.VMEM((WORD_BYTES * SPAN, cycle), jnp.bfloat16),
                pltpu.SemaphoreType.REGULAR,
                pltpu.SemaphoreType.DMA,
                pltpu.SemaphoreType.DMA,
                pltpu.SemaphoreType.DMA,
                pltpu.SemaphoreType.DMA((LEVELS,)),
            ],
            compiler_params=pltpu.CompilerParams(
                collective_id=0, has_side_effects=True
            ),
        )(*(pltpu.with_memory_space_constraint(x, pltpu.HBM) for x in (assignment, database, queries, key_rows, hint)))

    placed = (P("col", "grp"), P("grp", "col"), P("grp", "col"), P("grp", None), P("grp"))
    return jax.shard_map(
        on_device,
        mesh=mesh,
        in_specs=placed,
        out_specs=P(("grp", "col"), None, None),
        check_vma=False,
    )
```

```python
import functools

import jax
import jax.numpy as jnp
from jax import lax
from jax.experimental import pallas as pl
from jax.experimental.pallas import tpu as pltpu
from jax.sharding import PartitionSpec as P

LEVELS = 2
DIGITS = 2
LANES = 128
WORD_BYTES = 4
DIGIT_BYTES = WORD_BYTES // DIGITS
SPAN = LANES // DIGIT_BYTES


def iota(shape, axis):
    return lax.broadcasted_iota(jnp.int32, shape, axis)


def byte_of(words, index):
    return jnp.bitwise_and(jnp.right_shift(words, 8 * index), 255).astype(jnp.float32)


def shifted(poly, amount):
    rows = poly.shape[0]
    amount = amount % (2 * rows * LANES)
    negate, turn = divmod(amount // LANES, rows)
    moved = poly
    if turn:
        moved = pltpu.roll(poly, turn, 0)
        moved = jnp.where(iota(poly.shape, 0) >= turn, moved, -moved)
    return -moved if negate else moved


def automorph(poly, level):
    step = poly.shape[0] * LANES >> level
    period = 2 << level
    residue = jnp.bitwise_and(iota(poly.shape, 1), period - 1)
    out = poly
    for m in range(1, period):
        out = jnp.where(residue == m, shifted(poly, step * m), out)
    return out


def fill_toeplitz(word_poly, toeplitz):
    rows = word_poly.shape[0]
    block = (SPAN, LANES)
    ahead = iota(block, 1) >= iota(block, 0)

    def turned(q):
        row = jnp.broadcast_to(word_poly[q : q + 1], block)
        return pltpu.roll(row, 0, 1, stride=1, stride_axis=0)

    before = turned(rows - 1)
    for q in range(rows):
        here = turned(q)
        words = jnp.where(ahead, here, before)
        for b in range(WORD_BYTES):
            part = byte_of(words, b)
            if q == 0:
                part = jnp.where(ahead, part, -part)
            toeplitz[b * SPAN : (b + 1) * SPAN, q * LANES : (q + 1) * LANES] = part.astype(
                jnp.bfloat16
            )
        before = here


def spread(tile):
    first = iota(tile.shape, 1) < SPAN
    turned = pltpu.roll(tile, SPAN, 1)
    return [
        jnp.where(first, tile, jnp.left_shift(turned, 8)),
        jnp.where(first, turned, jnp.left_shift(tile, 8)),
    ]


def key_side(keys):
    blocks = []
    for s in range(WORD_BYTES):
        for p in range(len(keys[0])):
            for h in range(DIGIT_BYTES):
                tiles = [byte_of(digit_keys[p][h], s) for digit_keys in keys]
                blocks.append(jnp.concatenate(tiles, axis=1))
    return jnp.concatenate(blocks, axis=0).astype(jnp.bfloat16)


def switch(toeplitz, key_polys, rows):
    sides = len(key_polys[0])
    products = jnp.dot(
        key_side(key_polys), toeplitz, preferred_element_type=jnp.float32
    ).astype(jnp.int32)
    lane = iota((rows, LANES), 1)
    sums = []
    for p in range(sides):
        total = jnp.zeros((rows, LANES), jnp.int32)
        for h in range(DIGIT_BYTES):
            words = None
            for s in range(WORD_BYTES):
                at = ((s * sides + p) * DIGIT_BYTES + h) * rows
                term = jnp.left_shift(products[at : at + rows], 8 * s)
                words = term if words is None else words + term
            out = words[:, :LANES]
            for q in range(1, rows):
                out = out + shifted(words[:, q * LANES : (q + 1) * LANES], q * LANES)
            if h:
                turn = h * SPAN
                carried = pltpu.roll(shifted(out, LANES), turn, 1)
                out = jnp.where(lane >= turn, pltpu.roll(out, turn, 1), carried)
            total = total + out
        sums.append(total)
    return sums


def kernel(
    n, slots, share, width, assign_hbm, database_hbm, queries_hbm, keys_hbm, hint_hbm, out,
    assign, database, queries, keys, hint, loaded, unit_part, unit_keys, masks,
    ans_send, key_send, ans_recv, key_recv, key_words, toeplitz,
    ready, ans_got, key_got,
):
    me = lax.axis_index("col")
    clients, columns = queries.shape
    polys, cycle = hint.shape
    rows = cycle // LANES
    key_rows = key_send.shape[1] // slots
    key_pitch = unit_keys.shape[1]
    unit_key_rows = unit_keys.reshape(clients * polys * key_pitch, LANES)
    unit_part_rows = unit_part.reshape(clients * polys * rows, LANES)
    chunks = 4
    chunk = database.shape[1] // chunks
    size = 2
    planes = n // size
    few = n <= LANES // 8
    level_blocks = n // LEVELS
    chip = lax.div(me, size)
    partner = me + 1 - 2 * lax.rem(me, size)
    height = planes // width
    across = lax.rem(chip, width)
    along = lax.div(chip, width)
    poly_blocks = n // (LEVELS * DIGITS * 2)
    kind_held = jnp.where(me >= n - poly_blocks, LEVELS, lax.div(me, level_blocks))

    def each(count, body, start=0):
        lax.fori_loop(start, count, lambda i, c: (body(i), c)[1], 0, unroll=few)
    loads = [
        pltpu.make_async_copy(source, target, loaded.at[min(i, 2)])
        for i, (source, target) in enumerate(
            (
                (assign_hbm, assign),
                (keys_hbm, keys),
                (queries_hbm, queries),
                (database_hbm, database),
                (hint_hbm, hint),
            )
        )
    ]
    for i, load in enumerate(loads):
        if i == 3:
            for j in range(chunks):
                at = pl.ds(j * chunk, chunk)
                pltpu.make_async_copy(database_hbm.at[:, at], database.at[:, at], loaded.at[2]).start()
        else:
            load.start()
    def span(start, stop, body):
        lax.fori_loop(start, stop, lambda i, c: (body(i), c)[1], 0)

    def on_chips(start, stop, column, body):
        def both(i):
            first = (i * width + column) * size
            for core in range(size):
                body(first + core)

        span(start, stop, both)

    sent = loaded.at[0]
    barrier = pltpu.get_barrier_semaphore()

    def greet(there):
        pl.semaphore_signal(barrier, inc=1, device_id={"col": there})

    greet(partner)
    for column in range(width):
        on_chips(
            jnp.where(column < across, height, along + jnp.where(column == across, 1, 0)),
            height,
            column,
            greet,
        )
    pl.semaphore_wait(barrier, (along + 1) * (across + 1) * size - 1)

    def announce(stage, chips):
        @pl.when(chip == chips - 1)
        def _():
            def tell(i):
                there = i * size + lax.rem(me, size)
                pl.semaphore_signal(ready.at[stage], inc=1, device_id={"col": there})

            span(0, chips - 1, tell)

    announce(0, planes // 2)
    announce(1, planes)
    loads[0].wait()
    loads[1].wait()
    lane_owner = iota((clients, LANES), 1) // (LANES // share)
    for j in range(key_rows):
        tile = keys[:, j * LANES : (j + 1) * LANES]
        if share > 1:
            tile = jnp.where(lane_owner == lax.rem(me, share), tile, 0)
        for p in range(polys):
            unit_key_rows[pl.ds(p * key_pitch + j, clients, stride=polys * key_pitch), :] = tile

    def stage_keys(owner):
        for k in range(slots):
            key_send[owner, k * key_rows : (k + 1) * key_rows, :] = unit_keys[assign[owner * slots + k]][:key_rows]

    def stage_answers(owner):
        for k in range(slots):
            ans_send[owner, k * rows : (k + 1) * rows, :] = unit_part[assign[owner * slots + k]]
    each(n, stage_keys)

    def send_keys(there):
        pltpu.make_async_remote_copy(
            src_ref=key_send.at[there],
            dst_ref=key_recv.at[me],
            send_sem=sent,
            recv_sem=key_got.at[kind_held],
            device_id={"col": there},
        ).start()

    def send_answers(there):
        pltpu.make_async_remote_copy(
            src_ref=ans_send.at[there],
            dst_ref=ans_recv.at[me],
            send_sem=sent,
            recv_sem=ans_got,
            device_id={"col": there},
        ).start()

    def to_first(send):
        @pl.when(chip > 0)
        def _():
            for core in range(size):
                send(core)

    def to_early(send):
        for column in range(width):
            on_chips(
                0 if column else 1,
                jnp.where(column > across, 0, along + jnp.where(column == across, 0, 1)),
                column,
                send,
            )
        send(partner)

    def to_late(stage, send):
        for column in range(width):
            start = jnp.where(column > across, 0, along + 1)
            if stage:
                start = jnp.maximum(start, jnp.where(along < height // 2, height // 2, 0))
            on_chips(start, height // 2 if stage == 0 else height, column, send)
    to_first(send_keys)
    pltpu.make_async_copy(key_send.at[me], key_recv.at[me], key_got.at[kind_held]).start()
    for load in loads[2:]:
        load.wait()
    query_words = queries[...]
    query_bytes = jnp.concatenate(
        [byte_of(query_words, b) for b in range(WORD_BYTES)], axis=0
    ).astype(jnp.bfloat16)
    products = jnp.dot(
        query_bytes,
        database[...].astype(jnp.float32).astype(jnp.bfloat16),
        preferred_element_type=jnp.float32,
    ).astype(jnp.int32)
    partial = products[:clients]
    for b in range(1, WORD_BYTES):
        partial = partial + jnp.left_shift(products[b * clients : (b + 1) * clients], 8 * b)
    for j in range(polys * rows):
        unit_part_rows[pl.ds(j, clients, stride=polys * rows), :] = partial[:, j * LANES : (j + 1) * LANES]
    each(n, stage_answers)
    to_first(send_answers)
    to_early(send_keys)
    to_early(send_answers)
    pltpu.make_async_copy(ans_send.at[me], ans_recv.at[me], ans_got).start()
    for p in range(polys):
        for q in range(rows):
            masks[p, q : q + 1, :] = hint[p : p + 1, q * LANES : (q + 1) * LANES]

    def first_mask(k):
        return masks[lax.rem(assign[me * slots + k], polys)]

    fill_toeplitz(automorph(first_mask(0), 0), toeplitz)
    def when_ready(stage, chips):
        @pl.when((along < chips // width) & (chip != chips - 1))
        def _():
            pl.semaphore_wait(ready.at[stage], 1)
            to_late(stage, send_keys)
            to_late(stage, send_answers)

    when_ready(0, planes // 2)

    when_ready(1, planes)

    def wait_blocks(buffer, semaphore, start, count):
        blocks = buffer.at[pl.ds(start, count)]
        pltpu.make_async_copy(blocks, blocks, semaphore).wait()
    switched = []

    def gather_keys(k, kind, start, stop):
        if k == 0:
            wait_blocks(key_recv, key_got.at[kind], start, stop - start)
        for j in range(start // share, stop // share):
            block = key_recv[j * share, k * key_rows : (k + 1) * key_rows, :]
            for i in range(1, share):
                block = block + key_recv[j * share + i, k * key_rows : (k + 1) * key_rows, :]
            key_words[j * key_rows : (j + 1) * key_rows, :] = block

    def key_poly(level, t, p):
        at = ((level * DIGITS + t) * 2 + p) * rows
        return spread(key_words[at : at + rows, :])

    for k in range(slots):
        mask = first_mask(k)
        if k:
            fill_toeplitz(automorph(mask, 0), toeplitz)
        added = []
        for level in range(LEVELS):
            if level:
                fill_toeplitz(automorph(mask, level), toeplitz)
            last = level == LEVELS - 1
            stop = (level + 1) * level_blocks
            gather_keys(k, level, level * level_blocks, stop - (poly_blocks if last else 0))
            polys_held = [[key_poly(level, t, p) for p in range(2)] for t in range(DIGITS)]
            if last:
                zero = jnp.zeros((rows, LANES), jnp.int32)
                polys_held[-1][-1] = [zero] * DIGIT_BYTES
            to_mask, to_value = switch(toeplitz[...], polys_held, rows)
            mask = mask + to_mask
            if last:
                gather_keys(k, LEVELS, stop - poly_blocks, stop)
                tail = switch(toeplitz[-DIGIT_BYTES * SPAN :, :], [[key_poly(level, DIGITS - 1, 1)]], rows)
                to_value = to_value + tail[0]
            added.append(to_value)
        switched.append((mask, added))
    wait_blocks(ans_recv, ans_got, 0, n)
    for k, (mask, added) in enumerate(switched):
        value = ans_recv[0, k * rows : (k + 1) * rows, :]
        for j in range(1, n):
            value = value + ans_recv[j, k * rows : (k + 1) * rows, :]
        for level in range(LEVELS):
            value = value + automorph(value, level) + added[level]
        for index, words in enumerate((mask, value)):
            scaled = words.astype(jnp.float32) * 2.0 ** (-32)
            for q in range(rows):
                out[k, index : index + 1, q * LANES : (q + 1) * LANES] = scaled[q : q + 1]
    wait_blocks(key_send, sent, 0, n - 1)
    wait_blocks(ans_send, sent, 0, n - 1)


def solution(mesh):
    n = mesh.shape["col"]
    across = 2

    def on_device(database, queries, key_rows, hint, assignment):
        clients = queries.shape[0]
        polys, cycle = hint.shape
        rows = cycle // LANES
        slots = assignment.shape[0] // n
        width = key_rows.shape[1]
        share = max(1, LANES // width)
        if share > 1:
            key_rows = jnp.tile(key_rows, (1, share))
        tiles = key_rows.shape[1] // LANES
        place = pl.BlockSpec(memory_space=pltpu.HBM)
        return pl.pallas_call(
            functools.partial(kernel, n, slots, share, across),
            out_shape=pltpu.VMEM((slots, 2, cycle), jnp.float32),
            in_specs=[place] * 5,
            out_specs=pl.BlockSpec(memory_space=pltpu.VMEM),
            scratch_shapes=[
                pltpu.SMEM(assignment.shape, jnp.int32),
                pltpu.VMEM(database.shape, jnp.int32),
                pltpu.VMEM(queries.shape, jnp.int32),
                pltpu.VMEM(key_rows.shape, jnp.int32),
                pltpu.VMEM(hint.shape, jnp.int32),
                pltpu.SemaphoreType.DMA((3,)),
                pltpu.VMEM((polys * clients, rows, LANES), jnp.int32),
                pltpu.VMEM((polys * clients, -(-tiles // 8) * 8, LANES), jnp.int32),
                pltpu.VMEM((polys, rows, LANES), jnp.int32),
                pltpu.VMEM((n, slots * rows, LANES), jnp.int32),
                pltpu.VMEM((n, slots * tiles, LANES), jnp.int32),
                pltpu.VMEM((n, slots * rows, LANES), jnp.int32),
                pltpu.VMEM((n, slots * tiles, LANES), jnp.int32),
                pltpu.VMEM((n // share * tiles, LANES), jnp.int32),
                pltpu.VMEM((WORD_BYTES * SPAN, cycle), jnp.bfloat16),
                pltpu.SemaphoreType.REGULAR((2,)),
                pltpu.SemaphoreType.DMA,
                pltpu.SemaphoreType.DMA((LEVELS + 1,)),
            ],
            compiler_params=pltpu.CompilerParams(
                collective_id=0, has_side_effects=True
            ),
        )(*(pltpu.with_memory_space_constraint(x, pltpu.HBM) for x in (assignment, database, queries, key_rows, hint)))

    placed = (P("col", "grp"), P("grp", "col"), P("grp", "col"), P("grp", None), P("grp"))
    return jax.shard_map(
        on_device,
        mesh=mesh,
        in_specs=placed,
        out_specs=P(("grp", "col"), None, None),
        check_vma=False,
    )
```

```python
import functools

import jax
import jax.numpy as jnp
from jax import lax
from jax.experimental import pallas as pl
from jax.experimental.pallas import tpu as pltpu
from jax.sharding import PartitionSpec as P

LEVELS = 2
DIGITS = 2
LANES = 128
WORD_BYTES = 4
DIGIT_BYTES = WORD_BYTES // DIGITS
SPAN = LANES // DIGIT_BYTES


def iota(shape, axis):
    return lax.broadcasted_iota(jnp.int32, shape, axis)


def byte_of(words, index):
    return jnp.bitwise_and(jnp.right_shift(words, 8 * index), 255).astype(jnp.float32)


def shifted(poly, amount):
    rows = poly.shape[0]
    amount = amount % (2 * rows * LANES)
    negate, turn = divmod(amount // LANES, rows)
    moved = poly
    if turn:
        moved = pltpu.roll(poly, turn, 0)
        moved = jnp.where(iota(poly.shape, 0) >= turn, moved, -moved)
    return -moved if negate else moved


def automorph(poly, level):
    step = poly.shape[0] * LANES >> level
    period = 2 << level
    residue = jnp.bitwise_and(iota(poly.shape, 1), period - 1)
    out = poly
    for m in range(1, period):
        out = jnp.where(residue == m, shifted(poly, step * m), out)
    return out


def fill_rows(word_poly, table, offset, placed):
    rows = word_poly.shape[0]
    block = (SPAN, LANES)
    ahead = iota(block, 1) >= iota(block, 0) + offset

    def turned(q):
        row = jnp.broadcast_to(word_poly[q : q + 1], block)
        return pltpu.roll(row, offset, 1, stride=1, stride_axis=0)

    before = turned(rows - 1)
    for q in range(rows):
        here = turned(q)
        words = jnp.where(ahead, here, before)
        for b, at in placed:
            part = byte_of(words, b)
            if q == 0:
                part = jnp.where(ahead, part, -part)
            table[at : at + SPAN, q * LANES : (q + 1) * LANES] = part.astype(jnp.bfloat16)
        before = here


def fill_toeplitz(word_poly, toeplitz):
    fill_rows(word_poly, toeplitz, 0, [(b, b * SPAN) for b in range(WORD_BYTES)])


def fill_tail(word_poly, table):
    for offset in range(0, LANES, SPAN):
        fill_rows(
            word_poly,
            table,
            offset,
            [((DIGITS - 1) * DIGIT_BYTES + a, a * LANES + offset) for a in range(DIGIT_BYTES)],
        )


def spread(tile):
    first = iota(tile.shape, 1) < SPAN
    turned = pltpu.roll(tile, SPAN, 1)
    return [
        jnp.where(first, tile, jnp.left_shift(turned, 8)),
        jnp.where(first, turned, jnp.left_shift(tile, 8)),
    ]


def key_side(keys):
    blocks = []
    for s in range(WORD_BYTES):
        for p in range(len(keys[0])):
            for h in range(DIGIT_BYTES):
                tiles = [byte_of(digit_keys[p][h], s) for digit_keys in keys]
                blocks.append(jnp.concatenate(tiles, axis=1))
    return jnp.concatenate(blocks, axis=0).astype(jnp.bfloat16)


def switch(toeplitz, key_polys, rows):
    sides = len(key_polys[0])
    products = jnp.dot(
        key_side(key_polys), toeplitz, preferred_element_type=jnp.float32
    ).astype(jnp.int32)
    lane = iota((rows, LANES), 1)
    sums = []
    for p in range(sides):
        total = jnp.zeros((rows, LANES), jnp.int32)
        for h in range(DIGIT_BYTES):
            words = None
            for s in range(WORD_BYTES):
                at = ((s * sides + p) * DIGIT_BYTES + h) * rows
                term = jnp.left_shift(products[at : at + rows], 8 * s)
                words = term if words is None else words + term
            out = words[:, :LANES]
            for q in range(1, rows):
                out = out + shifted(words[:, q * LANES : (q + 1) * LANES], q * LANES)
            if h:
                turn = h * SPAN
                carried = pltpu.roll(shifted(out, LANES), turn, 1)
                out = jnp.where(lane >= turn, pltpu.roll(out, turn, 1), carried)
            total = total + out
        sums.append(total)
    return sums


def switch_tail(table, words):
    rows = words.shape[0]
    moved = [jnp.left_shift(words, 8 * a) for a in range(DIGIT_BYTES)]
    side = jnp.concatenate(
        [
            jnp.concatenate([byte_of(part, s) for part in moved], axis=1)
            for s in range(WORD_BYTES)
        ],
        axis=0,
    ).astype(jnp.bfloat16)
    products = jnp.dot(side, table, preferred_element_type=jnp.float32).astype(jnp.int32)
    total = products[:rows]
    for s in range(1, WORD_BYTES):
        total = total + jnp.left_shift(products[s * rows : (s + 1) * rows], 8 * s)
    out = total[:, :LANES]
    for q in range(1, rows):
        out = out + shifted(total[:, q * LANES : (q + 1) * LANES], q * LANES)
    return out


def kernel(
    n, slots, share, width, assign_hbm, database_hbm, queries_hbm, keys_hbm, hint_hbm, out,
    assign, database, queries, keys, hint, loaded, unit_part, unit_keys, masks,
    ans_send, key_send, ans_recv, key_recv, key_words, toeplitz, tail, held,
    ready, ans_got, key_got,
):
    me = lax.axis_index("col")
    clients, columns = queries.shape
    polys, cycle = hint.shape
    rows = cycle // LANES
    key_rows = key_send.shape[1] // slots
    key_pitch = unit_keys.shape[1]
    unit_key_rows = unit_keys.reshape(clients * polys * key_pitch, LANES)
    unit_part_rows = unit_part.reshape(clients * polys * rows, LANES)
    chunks = 4
    chunk = database.shape[1] // chunks
    size = 2
    planes = n // size
    few = n <= LANES // 8
    level_blocks = n // LEVELS
    chip = lax.div(me, size)
    partner = me + 1 - 2 * lax.rem(me, size)
    height = planes // width
    across = lax.rem(chip, width)
    along = lax.div(chip, width)
    poly_blocks = n // (LEVELS * DIGITS * 2)
    kind_held = jnp.where(me >= n - poly_blocks, LEVELS, lax.div(me, level_blocks))

    def each(count, body, start=0):
        lax.fori_loop(start, count, lambda i, c: (body(i), c)[1], 0, unroll=few)
    loads = [
        pltpu.make_async_copy(source, target, loaded.at[min(i // 2, 1)])
        for i, (source, target) in enumerate(
            (
                (assign_hbm, assign),
                (keys_hbm, keys),
                (database_hbm, database),
                (queries_hbm, queries),
                (hint_hbm, hint),
            )
        )
    ]
    for i, load in enumerate(loads):
        if i == 2:
            for j in range(chunks):
                at = pl.ds(j * chunk, chunk)
                pltpu.make_async_copy(database_hbm.at[:, at], database.at[:, at], loaded.at[1]).start()
        else:
            load.start()
    def span(start, stop, body):
        lax.fori_loop(start, stop, lambda i, c: (body(i), c)[1], 0)

    def on_chips(start, stop, column, body):
        def both(i):
            first = (i * width + column) * size
            for core in range(size):
                body(first + core)

        span(start, stop, both)

    sent = loaded.at[0]
    barrier = pltpu.get_barrier_semaphore()

    def greet(there):
        pl.semaphore_signal(barrier, inc=1, device_id={"col": there})

    greet(partner)
    for column in range(width):
        on_chips(
            jnp.where(column < across, height, along + jnp.where(column == across, 1, 0)),
            height,
            column,
            greet,
        )
    pl.semaphore_wait(barrier, (along + 1) * (across + 1) * size - 1)

    def announce(stage, chips):
        @pl.when(chip == chips - 1)
        def _():
            def tell(i):
                there = i * size + lax.rem(me, size)
                pl.semaphore_signal(ready.at[stage], inc=1, device_id={"col": there})

            span(0, chips - 1, tell)

    announce(0, planes // 2)
    announce(1, planes)
    loads[0].wait()
    loads[1].wait()
    lane_owner = iota((clients, LANES), 1) // (LANES // share)
    for j in range(key_rows):
        tile = keys[:, j * LANES : (j + 1) * LANES]
        if share > 1:
            tile = jnp.where(lane_owner == lax.rem(me, share), tile, 0)
        for p in range(polys):
            unit_key_rows[pl.ds(p * key_pitch + j, clients, stride=polys * key_pitch), :] = tile

    def stage_keys(owner):
        for k in range(slots):
            key_send[owner, k * key_rows : (k + 1) * key_rows, :] = unit_keys[assign[owner * slots + k]][:key_rows]

    def stage_answers(owner):
        for k in range(slots):
            ans_send[owner, k * rows : (k + 1) * rows, :] = unit_part[assign[owner * slots + k]]
    each(n, stage_keys)

    def send_keys(there):
        pltpu.make_async_remote_copy(
            src_ref=key_send.at[there],
            dst_ref=key_recv.at[me],
            send_sem=sent,
            recv_sem=key_got.at[kind_held],
            device_id={"col": there},
        ).start()

    def send_answers(there):
        pltpu.make_async_remote_copy(
            src_ref=ans_send.at[there],
            dst_ref=ans_recv.at[me],
            send_sem=sent,
            recv_sem=ans_got,
            device_id={"col": there},
        ).start()

    def to_first(send):
        @pl.when(chip > 0)
        def _():
            for core in range(size):
                send(core)

    def to_early(send):
        for column in range(width):
            on_chips(
                0 if column else 1,
                jnp.where(column > across, 0, along + jnp.where(column == across, 0, 1)),
                column,
                send,
            )
        send(partner)

    def to_late(stage, send):
        for column in range(width):
            start = jnp.where(column > across, 0, along + 1)
            if stage:
                start = jnp.maximum(start, jnp.where(along < height // 2, height // 2, 0))
            on_chips(start, height // 2 if stage == 0 else height, column, send)
    to_first(send_keys)
    pltpu.make_async_copy(key_send.at[me], key_recv.at[me], key_got.at[kind_held]).start()
    for load in loads[2:]:
        load.wait()
    query_words = queries[...]
    query_bytes = jnp.concatenate(
        [byte_of(query_words, b) for b in range(WORD_BYTES)], axis=0
    ).astype(jnp.bfloat16)
    products = jnp.dot(
        query_bytes,
        database[...].astype(jnp.float32).astype(jnp.bfloat16),
        preferred_element_type=jnp.float32,
    ).astype(jnp.int32)
    partial = products[:clients]
    for b in range(1, WORD_BYTES):
        partial = partial + jnp.left_shift(products[b * clients : (b + 1) * clients], 8 * b)
    for j in range(polys * rows):
        unit_part_rows[pl.ds(j, clients, stride=polys * rows), :] = partial[:, j * LANES : (j + 1) * LANES]
    for core in range(size):
        stage_answers(core)
    to_first(send_answers)
    each(n, stage_answers, size)
    to_early(send_keys)
    to_early(send_answers)
    pltpu.make_async_copy(ans_send.at[me], ans_recv.at[me], ans_got).start()
    for p in range(polys):
        for q in range(rows):
            masks[p, q : q + 1, :] = hint[p : p + 1, q * LANES : (q + 1) * LANES]

    def first_mask(k):
        return masks[lax.rem(assign[me * slots + k], polys)]

    fill_toeplitz(automorph(first_mask(0), 0), toeplitz)
    def when_ready(stage, chips):
        @pl.when((along < chips // width) & (chip != chips - 1))
        def _():
            pl.semaphore_wait(ready.at[stage], 1)
            to_late(stage, send_keys)
            to_late(stage, send_answers)

    when_ready(0, planes // 2)

    when_ready(1, planes)

    def wait_blocks(buffer, semaphore, start, count):
        blocks = buffer.at[pl.ds(start, count)]
        pltpu.make_async_copy(blocks, blocks, semaphore).wait()
    switched = []

    def gather_keys(k, kind, start, stop):
        if k == 0:
            wait_blocks(key_recv, key_got.at[kind], start, stop - start)
        for j in range(start // share, stop // share):
            block = key_recv[j * share, k * key_rows : (k + 1) * key_rows, :]
            for i in range(1, share):
                block = block + key_recv[j * share + i, k * key_rows : (k + 1) * key_rows, :]
            key_words[j * key_rows : (j + 1) * key_rows, :] = block

    def key_poly(level, t, p):
        at = ((level * DIGITS + t) * 2 + p) * rows
        return key_words[at : at + rows, :]

    def key_polys(level):
        return [[spread(key_poly(level, t, p)) for p in range(2)] for t in range(DIGITS)]

    last = LEVELS - 1
    for k in range(slots):
        mask = first_mask(k)
        if k:
            fill_toeplitz(automorph(mask, 0), toeplitz)
        added = []
        for level in range(last):
            gather_keys(k, level, level * level_blocks, (level + 1) * level_blocks)
            to_mask, to_value = switch(toeplitz[...], key_polys(level), rows)
            mask = mask + to_mask
            added.append(to_value)
            turned = automorph(mask, level + 1)
            fill_toeplitz(turned, toeplitz)
        early, late = n - level_blocks, n - poly_blocks
        @pl.when(chip > 0)
        def _():
            gather_keys(k, last, early, late)
            gather_keys(k, LEVELS, late, n)
            to_mask, to_value = switch(toeplitz[...], key_polys(last), rows)
            held[k, 0] = mask + to_mask
            held[k, 1] = to_value

        @pl.when(chip == 0)
        def _():
            gather_keys(k, last, early, late)
            polys_held = key_polys(last)
            polys_held[-1][-1] = [jnp.zeros((rows, LANES), jnp.int32)] * DIGIT_BYTES
            to_mask, to_value = switch(toeplitz[...], polys_held, rows)
            held[k, 0] = mask + to_mask
            fill_tail(turned, tail)
            gather_keys(k, LEVELS, late, n)
            held[k, 1] = to_value + switch_tail(tail[...], key_poly(last, DIGITS - 1, 1))

        switched.append(added)
    wait_blocks(ans_recv, ans_got, 0, n)
    for k, added in enumerate(switched):
        mask = held[k, 0]
        added = added + [held[k, 1]]
        value = ans_recv[0, k * rows : (k + 1) * rows, :]
        for j in range(1, n):
            value = value + ans_recv[j, k * rows : (k + 1) * rows, :]
        for level in range(LEVELS):
            value = value + automorph(value, level) + added[level]
        for index, words in enumerate((mask, value)):
            scaled = words.astype(jnp.float32) * 2.0 ** (-32)
            for q in range(rows):
                out[k, index : index + 1, q * LANES : (q + 1) * LANES] = scaled[q : q + 1]
    wait_blocks(key_send, sent, 0, n - 1)
    wait_blocks(ans_send, sent, 0, n - 1)


def solution(mesh):
    n = mesh.shape["col"]
    across = 2

    def on_device(database, queries, key_rows, hint, assignment):
        clients = queries.shape[0]
        polys, cycle = hint.shape
        rows = cycle // LANES
        slots = assignment.shape[0] // n
        width = key_rows.shape[1]
        share = max(1, LANES // width)
        if share > 1:
            key_rows = jnp.tile(key_rows, (1, share))
        tiles = key_rows.shape[1] // LANES
        place = pl.BlockSpec(memory_space=pltpu.HBM)
        return pl.pallas_call(
            functools.partial(kernel, n, slots, share, across),
            out_shape=pltpu.VMEM((slots, 2, cycle), jnp.float32),
            in_specs=[place] * 5,
            out_specs=pl.BlockSpec(memory_space=pltpu.VMEM),
            scratch_shapes=[
                pltpu.SMEM(assignment.shape, jnp.int32),
                pltpu.VMEM(database.shape, jnp.int32),
                pltpu.VMEM(queries.shape, jnp.int32),
                pltpu.VMEM(key_rows.shape, jnp.int32),
                pltpu.VMEM(hint.shape, jnp.int32),
                pltpu.SemaphoreType.DMA((2,)),
                pltpu.VMEM((polys * clients, rows, LANES), jnp.int32),
                pltpu.VMEM((polys * clients, -(-tiles // 8) * 8, LANES), jnp.int32),
                pltpu.VMEM((polys, rows, LANES), jnp.int32),
                pltpu.VMEM((n, slots * rows, LANES), jnp.int32),
                pltpu.VMEM((n, slots * tiles, LANES), jnp.int32),
                pltpu.VMEM((n, slots * rows, LANES), jnp.int32),
                pltpu.VMEM((n, slots * tiles, LANES), jnp.int32),
                pltpu.VMEM((n // share * tiles, LANES), jnp.int32),
                pltpu.VMEM((WORD_BYTES * SPAN, cycle), jnp.bfloat16),
                pltpu.VMEM((DIGIT_BYTES * LANES, cycle), jnp.bfloat16),
                pltpu.VMEM((slots, 2, rows, LANES), jnp.int32),
                pltpu.SemaphoreType.REGULAR((2,)),
                pltpu.SemaphoreType.DMA,
                pltpu.SemaphoreType.DMA((LEVELS + 1,)),
            ],
            compiler_params=pltpu.CompilerParams(
                collective_id=0, has_side_effects=True
            ),
        )(*(pltpu.with_memory_space_constraint(x, pltpu.HBM) for x in (assignment, database, queries, key_rows, hint)))

    placed = (P("col", "grp"), P("grp", "col"), P("grp", "col"), P("grp", None), P("grp"))
    return jax.shard_map(
        on_device,
        mesh=mesh,
        in_specs=placed,
        out_specs=P(("grp", "col"), None, None),
        check_vma=False,
    )
```

```python
import functools

import jax
import jax.numpy as jnp
from jax import lax
from jax.experimental import pallas as pl
from jax.experimental.pallas import tpu as pltpu
from jax.sharding import PartitionSpec as P

LEVELS = 2
DIGITS = 2
LANES = 128
WORD_BYTES = 4
DIGIT_BYTES = WORD_BYTES // DIGITS
SPAN = LANES // DIGIT_BYTES


def iota(shape, axis):
    return lax.broadcasted_iota(jnp.int32, shape, axis)


def byte_of(words, index):
    return jnp.bitwise_and(jnp.right_shift(words, 8 * index), 255).astype(jnp.float32)


def shifted(poly, amount):
    rows = poly.shape[0]
    amount = amount % (2 * rows * LANES)
    negate, turn = divmod(amount // LANES, rows)
    moved = poly
    if turn:
        moved = pltpu.roll(poly, turn, 0)
        moved = jnp.where(iota(poly.shape, 0) >= turn, moved, -moved)
    return -moved if negate else moved


def automorph(poly, level):
    step = poly.shape[0] * LANES >> level
    period = 2 << level
    residue = jnp.bitwise_and(iota(poly.shape, 1), period - 1)
    out = poly
    for m in range(1, period):
        out = jnp.where(residue == m, shifted(poly, step * m), out)
    return out


def fill_rows(word_poly, table, offset, placed):
    rows = word_poly.shape[0]
    block = (SPAN, LANES)
    ahead = iota(block, 1) >= iota(block, 0) + offset

    def turned(q):
        row = jnp.broadcast_to(word_poly[q : q + 1], block)
        return pltpu.roll(row, offset, 1, stride=1, stride_axis=0)

    before = turned(rows - 1)
    for q in range(rows):
        here = turned(q)
        words = jnp.where(ahead, here, before)
        for b, at in placed:
            part = byte_of(words, b)
            if q == 0:
                part = jnp.where(ahead, part, -part)
            table[at : at + SPAN, q * LANES : (q + 1) * LANES] = part.astype(jnp.bfloat16)
        before = here


def fill_toeplitz(word_poly, toeplitz):
    fill_rows(word_poly, toeplitz, 0, [(b, b * SPAN) for b in range(WORD_BYTES)])


def fill_tail(word_poly, table):
    for offset in range(0, LANES, SPAN):
        fill_rows(
            word_poly,
            table,
            offset,
            [((DIGITS - 1) * DIGIT_BYTES + a, a * LANES + offset) for a in range(DIGIT_BYTES)],
        )


def spread(tile):
    first = iota(tile.shape, 1) < SPAN
    turned = pltpu.roll(tile, SPAN, 1)
    return [
        jnp.where(first, tile, jnp.left_shift(turned, 8)),
        jnp.where(first, turned, jnp.left_shift(tile, 8)),
    ]


def key_side(keys):
    blocks = []
    for s in range(WORD_BYTES):
        for p in range(len(keys[0])):
            for h in range(DIGIT_BYTES):
                tiles = [byte_of(digit_keys[p][h], s) for digit_keys in keys]
                blocks.append(jnp.concatenate(tiles, axis=1))
    return jnp.concatenate(blocks, axis=0).astype(jnp.bfloat16)


def switch(toeplitz, key_polys, rows):
    sides = len(key_polys[0])
    products = jnp.dot(
        key_side(key_polys), toeplitz, preferred_element_type=jnp.float32
    ).astype(jnp.int32)
    lane = iota((rows, LANES), 1)
    sums = []
    for p in range(sides):
        total = jnp.zeros((rows, LANES), jnp.int32)
        for h in range(DIGIT_BYTES):
            words = None
            for s in range(WORD_BYTES):
                at = ((s * sides + p) * DIGIT_BYTES + h) * rows
                term = jnp.left_shift(products[at : at + rows], 8 * s)
                words = term if words is None else words + term
            out = words[:, :LANES]
            for q in range(1, rows):
                out = out + shifted(words[:, q * LANES : (q + 1) * LANES], q * LANES)
            if h:
                turn = h * SPAN
                carried = pltpu.roll(shifted(out, LANES), turn, 1)
                out = jnp.where(lane >= turn, pltpu.roll(out, turn, 1), carried)
            total = total + out
        sums.append(total)
    return sums


def switch_tail(table, words):
    rows = words.shape[0]
    moved = [jnp.left_shift(words, 8 * a) for a in range(DIGIT_BYTES)]
    side = jnp.concatenate(
        [
            jnp.concatenate([byte_of(part, s) for part in moved], axis=1)
            for s in range(WORD_BYTES)
        ],
        axis=0,
    ).astype(jnp.bfloat16)
    products = jnp.dot(side, table, preferred_element_type=jnp.float32).astype(jnp.int32)
    total = products[:rows]
    for s in range(1, WORD_BYTES):
        total = total + jnp.left_shift(products[s * rows : (s + 1) * rows], 8 * s)
    out = total[:, :LANES]
    for q in range(1, rows):
        out = out + shifted(total[:, q * LANES : (q + 1) * LANES], q * LANES)
    return out


def fold_tiles(tiles):
    line = iota(tiles[0].shape, 0)
    apart = len(tiles) // 2
    while apart:
        low = jnp.bitwise_and(line, apart) == 0
        folded = []
        for first, second in zip(tiles[:apart], tiles[apart:]):
            kept = jnp.where(low, first, second)
            other = jnp.where(low, second, first)
            down = pltpu.roll(other, apart, 0)
            if 2 * apart < line.shape[0]:
                down = jnp.where(low, pltpu.roll(other, line.shape[0] - apart, 0), down)
            folded.append(kept + down)
        tiles = folded
        apart //= 2
    return tiles[0]


def kernel(
    n, slots, share, width, assign_hbm, database_hbm, queries_hbm, keys_hbm, hint_hbm, out,
    assign, query_scalars, database, queries, keys, hint, loaded, unit_part, unit_keys, masks,
    ans_send, key_send, ans_recv, key_recv, key_words, toeplitz, tail, held,
    ready, ans_got, key_got,
):
    me = lax.axis_index("col")
    clients, columns = queries.shape
    polys, cycle = hint.shape
    rows = cycle // LANES
    key_rows = key_send.shape[1] // slots
    key_pitch = unit_keys.shape[1]
    unit_key_rows = unit_keys.reshape(clients * polys * key_pitch, LANES)
    unit_part_rows = unit_part.reshape(clients * polys * rows, LANES)
    pieces = max(1, 4 // polys)
    piece = cycle // pieces
    size = 2
    planes = n // size
    few = n <= LANES // 8
    level_blocks = n // LEVELS
    chip = lax.div(me, size)
    partner = me + 1 - 2 * lax.rem(me, size)
    height = planes // width
    across = lax.rem(chip, width)
    along = lax.div(chip, width)
    poly_blocks = n // (LEVELS * DIGITS * 2)
    kind_held = jnp.where(me >= n - poly_blocks, LEVELS, lax.div(me, level_blocks))

    def each(count, body, start=0):
        lax.fori_loop(start, count, lambda i, c: (body(i), c)[1], 0, unroll=few)
    loads = [
        pltpu.make_async_copy(source, target, loaded.at[i // 3])
        for i, (source, target) in enumerate(
            (
                (assign_hbm, assign),
                (queries_hbm, query_scalars),
                (keys_hbm, keys),
                (queries_hbm, queries),
                (hint_hbm, hint),
            )
        )
    ]
    for load in loads[:3]:
        load.start()
    for p in range(polys):
        for j in range(pieces):
            at = pl.ds(j * piece, piece)
            pltpu.make_async_copy(
                database_hbm.at[:, pl.ds(p * cycle + j * piece, piece)], database.at[p, :, at], loaded.at[1]
            ).start()
    for load in loads[3:]:
        load.start()
    def span(start, stop, body):
        lax.fori_loop(start, stop, lambda i, c: (body(i), c)[1], 0)

    def on_chips(start, stop, column, body):
        def both(i):
            first = (i * width + column) * size
            for core in range(size):
                body(first + core)

        span(start, stop, both)

    sent = loaded.at[0]
    barrier = pltpu.get_barrier_semaphore()

    def greet(there):
        pl.semaphore_signal(barrier, inc=1, device_id={"col": there})

    greet(partner)
    for column in range(width):
        on_chips(
            jnp.where(column < across, height, along + jnp.where(column == across, 1, 0)),
            height,
            column,
            greet,
        )
    pl.semaphore_wait(barrier, (along + 1) * (across + 1) * size - 1)

    def announce(stage, chips):
        @pl.when(chip == chips - 1)
        def _():
            def tell(i):
                there = i * size + lax.rem(me, size)
                pl.semaphore_signal(ready.at[stage], inc=1, device_id={"col": there})

            span(0, chips - 1, tell)

    announce(0, planes // 2)
    announce(1, planes)
    for load in loads[:3]:
        load.wait()
    lane_owner = iota((clients, LANES), 1) // (LANES // share)
    for j in range(key_rows):
        tile = keys[:, j * LANES : (j + 1) * LANES]
        if share > 1:
            tile = jnp.where(lane_owner == lax.rem(me, share), tile, 0)
        for p in range(polys):
            unit_key_rows[pl.ds(p * key_pitch + j, clients, stride=polys * key_pitch), :] = tile

    def stage_keys(owner):
        for k in range(slots):
            key_send[owner, k * key_rows : (k + 1) * key_rows, :] = unit_keys[assign[owner * slots + k]][:key_rows]

    def stage_answers(owner):
        for k in range(slots):
            ans_send[owner, k * rows : (k + 1) * rows, :] = unit_part[assign[owner * slots + k]]

    def send_keys(there):
        pltpu.make_async_remote_copy(
            src_ref=key_send.at[there],
            dst_ref=key_recv.at[me],
            send_sem=sent,
            recv_sem=key_got.at[kind_held],
            device_id={"col": there},
        ).start()

    def send_answers(there):
        pltpu.make_async_remote_copy(
            src_ref=ans_send.at[there],
            dst_ref=ans_recv.at[me],
            send_sem=sent,
            recv_sem=ans_got,
            device_id={"col": there},
        ).start()

    def to_first(send):
        @pl.when(chip > 0)
        def _():
            for core in range(size):
                send(core)

    def to_early(send):
        for column in range(width):
            on_chips(
                0 if column else 1,
                jnp.where(column > across, 0, along + jnp.where(column == across, 0, 1)),
                column,
                send,
            )
        send(partner)

    def to_late(stage, send):
        for column in range(width):
            start = jnp.where(column > across, 0, along + 1)
            if stage:
                start = jnp.maximum(start, jnp.where(along < height // 2, height // 2, 0))
            on_chips(start, height // 2 if stage == 0 else height, column, send)
    for core in range(size):
        stage_keys(core)
    to_first(send_keys)
    each(n, stage_keys, size)
    pltpu.make_async_copy(key_send.at[me], key_recv.at[me], key_got.at[kind_held]).start()

    line = iota((columns, LANES), 0)
    first_units = [assign[core * slots + k] for core in range(size) for k in range(slots)]
    first_queries = []
    for unit in first_units:
        client = lax.div(unit, polys)
        column = jnp.zeros((columns, LANES), jnp.int32)
        for j in range(columns):
            column = jnp.where(line == j, query_scalars[client, j], column)
        first_queries.append(column)
    pltpu.make_async_copy(database, database, loaded.at[1]).wait()
    for load in loads[3:]:
        load.wait()
    for i, (unit, column) in enumerate(zip(first_units, first_queries)):
        bytes_held = database[lax.rem(unit, polys)]
        tiles = []
        for q in range(rows):
            terms = bytes_held[:, q * LANES : (q + 1) * LANES] * column
            tile = terms[:rows]
            for j in range(rows, columns, rows):
                tile = tile + terms[j : j + rows]
            tiles.append(tile)
        core, k = divmod(i, slots)
        ans_send[core, k * rows : (k + 1) * rows, :] = fold_tiles(tiles)
    to_first(send_answers)
    query_words = queries[...]
    query_bytes = jnp.concatenate(
        [byte_of(query_words, b) for b in range(WORD_BYTES)], axis=0
    ).astype(jnp.bfloat16)
    for p in range(polys):
        products = jnp.dot(
            query_bytes,
            database[p].astype(jnp.float32).astype(jnp.bfloat16),
            preferred_element_type=jnp.float32,
        ).astype(jnp.int32)
        partial = products[:clients]
        for b in range(1, WORD_BYTES):
            partial = partial + jnp.left_shift(products[b * clients : (b + 1) * clients], 8 * b)
        for q in range(rows):
            rows_at = pl.ds(p * rows + q, clients, stride=polys * rows)
            unit_part_rows[rows_at, :] = partial[:, q * LANES : (q + 1) * LANES]
    each(n, stage_answers, size)
    to_early(send_keys)
    to_early(send_answers)
    pltpu.make_async_copy(ans_send.at[me], ans_recv.at[me], ans_got).start()
    for p in range(polys):
        for q in range(rows):
            masks[p, q : q + 1, :] = hint[p : p + 1, q * LANES : (q + 1) * LANES]

    def first_mask(k):
        return masks[lax.rem(assign[me * slots + k], polys)]

    fill_toeplitz(automorph(first_mask(0), 0), toeplitz)
    def when_ready(stage, chips):
        @pl.when((along < chips // width) & (chip != chips - 1))
        def _():
            pl.semaphore_wait(ready.at[stage], 1)
            to_late(stage, send_keys)
            to_late(stage, send_answers)

    when_ready(0, planes // 2)

    when_ready(1, planes)

    def wait_blocks(buffer, semaphore, start, count):
        blocks = buffer.at[pl.ds(start, count)]
        pltpu.make_async_copy(blocks, blocks, semaphore).wait()
    switched = []

    def gather_keys(k, kind, start, stop):
        if k == 0:
            wait_blocks(key_recv, key_got.at[kind], start, stop - start)
        for j in range(start // share, stop // share):
            block = key_recv[j * share, k * key_rows : (k + 1) * key_rows, :]
            for i in range(1, share):
                block = block + key_recv[j * share + i, k * key_rows : (k + 1) * key_rows, :]
            key_words[j * key_rows : (j + 1) * key_rows, :] = block

    def key_poly(level, t, p):
        at = ((level * DIGITS + t) * 2 + p) * rows
        return key_words[at : at + rows, :]

    def key_polys(level):
        return [[spread(key_poly(level, t, p)) for p in range(2)] for t in range(DIGITS)]

    last = LEVELS - 1
    for k in range(slots):
        mask = first_mask(k)
        if k:
            fill_toeplitz(automorph(mask, 0), toeplitz)
        added = []
        for level in range(last):
            gather_keys(k, level, level * level_blocks, (level + 1) * level_blocks)
            to_mask, to_value = switch(toeplitz[...], key_polys(level), rows)
            mask = mask + to_mask
            added.append(to_value)
            turned = automorph(mask, level + 1)
            fill_toeplitz(turned, toeplitz)
        early, late = n - level_blocks, n - poly_blocks
        @pl.when(chip > 0)
        def _():
            gather_keys(k, last, early, late)
            gather_keys(k, LEVELS, late, n)
            to_mask, to_value = switch(toeplitz[...], key_polys(last), rows)
            held[k, 0] = mask + to_mask
            held[k, 1] = to_value

        @pl.when(chip == 0)
        def _():
            gather_keys(k, last, early, late)
            polys_held = key_polys(last)
            polys_held[-1][-1] = [jnp.zeros((rows, LANES), jnp.int32)] * DIGIT_BYTES
            to_mask, to_value = switch(toeplitz[...], polys_held, rows)
            held[k, 0] = mask + to_mask
            fill_tail(turned, tail)
            gather_keys(k, LEVELS, late, n)
            held[k, 1] = to_value + switch_tail(tail[...], key_poly(last, DIGITS - 1, 1))

        switched.append(added)
    wait_blocks(ans_recv, ans_got, 0, n)
    for k, added in enumerate(switched):
        mask = held[k, 0]
        added = added + [held[k, 1]]
        value = ans_recv[0, k * rows : (k + 1) * rows, :]
        for j in range(1, n):
            value = value + ans_recv[j, k * rows : (k + 1) * rows, :]
        for level in range(LEVELS):
            value = value + automorph(value, level) + added[level]
        for index, words in enumerate((mask, value)):
            scaled = words.astype(jnp.float32) * 2.0 ** (-32)
            for q in range(rows):
                out[k, index : index + 1, q * LANES : (q + 1) * LANES] = scaled[q : q + 1]
    wait_blocks(key_send, sent, 0, n - 1)
    wait_blocks(ans_send, sent, 0, n - 1)


def solution(mesh):
    n = mesh.shape["col"]
    across = 2

    def on_device(database, queries, key_rows, hint, assignment):
        clients = queries.shape[0]
        polys, cycle = hint.shape
        rows = cycle // LANES
        slots = assignment.shape[0] // n
        width = key_rows.shape[1]
        share = max(1, LANES // width)
        if share > 1:
            key_rows = jnp.tile(key_rows, (1, share))
        tiles = key_rows.shape[1] // LANES
        place = pl.BlockSpec(memory_space=pltpu.HBM)
        return pl.pallas_call(
            functools.partial(kernel, n, slots, share, across),
            out_shape=pltpu.VMEM((slots, 2, cycle), jnp.float32),
            in_specs=[place] * 5,
            out_specs=pl.BlockSpec(memory_space=pltpu.VMEM),
            scratch_shapes=[
                pltpu.SMEM(assignment.shape, jnp.int32),
                pltpu.SMEM(queries.shape, jnp.int32),
                pltpu.VMEM((polys, database.shape[0], cycle), jnp.int32),
                pltpu.VMEM(queries.shape, jnp.int32),
                pltpu.VMEM(key_rows.shape, jnp.int32),
                pltpu.VMEM(hint.shape, jnp.int32),
                pltpu.SemaphoreType.DMA((2,)),
                pltpu.VMEM((polys * clients, rows, LANES), jnp.int32),
                pltpu.VMEM((polys * clients, -(-tiles // 8) * 8, LANES), jnp.int32),
                pltpu.VMEM((polys, rows, LANES), jnp.int32),
                pltpu.VMEM((n, slots * rows, LANES), jnp.int32),
                pltpu.VMEM((n, slots * tiles, LANES), jnp.int32),
                pltpu.VMEM((n, slots * rows, LANES), jnp.int32),
                pltpu.VMEM((n, slots * tiles, LANES), jnp.int32),
                pltpu.VMEM((n // share * tiles, LANES), jnp.int32),
                pltpu.VMEM((WORD_BYTES * SPAN, cycle), jnp.bfloat16),
                pltpu.VMEM((DIGIT_BYTES * LANES, cycle), jnp.bfloat16),
                pltpu.VMEM((slots, 2, rows, LANES), jnp.int32),
                pltpu.SemaphoreType.REGULAR((2,)),
                pltpu.SemaphoreType.DMA,
                pltpu.SemaphoreType.DMA((LEVELS + 1,)),
            ],
            compiler_params=pltpu.CompilerParams(
                collective_id=0, has_side_effects=True
            ),
        )(*(pltpu.with_memory_space_constraint(x, pltpu.HBM) for x in (assignment, database, queries, key_rows, hint)))

    placed = (P("col", "grp"), P("grp", "col"), P("grp", "col"), P("grp", None), P("grp"))
    return jax.shard_map(
        on_device,
        mesh=mesh,
        in_specs=placed,
        out_specs=P(("grp", "col"), None, None),
        check_vma=False,
    )
```

```python
import functools

import jax
import jax.numpy as jnp
from jax import lax
from jax.experimental import pallas as pl
from jax.experimental.pallas import tpu as pltpu
from jax.sharding import PartitionSpec as P

LEVELS = 2
DIGITS = 2
LANES = 128
WORD_BYTES = 4
DIGIT_BYTES = WORD_BYTES // DIGITS
SPAN = LANES // DIGIT_BYTES
MXUS = 2


def iota(shape, axis):
    return lax.broadcasted_iota(jnp.int32, shape, axis)


def byte_of(words, index):
    return jnp.bitwise_and(jnp.right_shift(words, 8 * index), 255).astype(jnp.float32)


def shifted(poly, amount):
    rows = poly.shape[0]
    amount = amount % (2 * rows * LANES)
    negate, turn = divmod(amount // LANES, rows)
    moved = poly
    if turn:
        moved = pltpu.roll(poly, turn, 0)
        moved = jnp.where(iota(poly.shape, 0) >= turn, moved, -moved)
    return -moved if negate else moved


def automorph(poly, level):
    step = poly.shape[0] * LANES >> level
    period = 2 << level
    residue = jnp.bitwise_and(iota(poly.shape, 1), period - 1)
    out = poly
    for m in range(1, period):
        out = jnp.where(residue == m, shifted(poly, step * m), out)
    return out


def fill_rows(word_poly, table, offset, placed):
    rows = word_poly.shape[0]
    block = (SPAN, LANES)
    ahead = iota(block, 1) >= iota(block, 0) + offset

    def turned(q):
        row = jnp.broadcast_to(word_poly[q : q + 1], block)
        return pltpu.roll(row, offset, 1, stride=1, stride_axis=0)

    before = turned(rows - 1)
    for q in range(rows):
        here = turned(q)
        words = jnp.where(ahead, here, before)
        for b, at in placed:
            part = byte_of(words, b)
            if q == 0:
                part = jnp.where(ahead, part, -part)
            table[at : at + SPAN, q * LANES : (q + 1) * LANES] = part.astype(jnp.bfloat16)
        before = here


def fill_toeplitz(word_poly, toeplitz):
    fill_rows(word_poly, toeplitz, 0, [(b, b * SPAN) for b in range(WORD_BYTES)])


def fill_tail(word_poly, table):
    for offset in range(0, LANES, SPAN):
        fill_rows(
            word_poly,
            table,
            offset,
            [((DIGITS - 1) * DIGIT_BYTES + a, a * LANES + offset) for a in range(DIGIT_BYTES)],
        )


def spread(tile):
    first = iota(tile.shape, 1) < SPAN
    turned = pltpu.roll(tile, SPAN, 1)
    return [
        jnp.where(first, tile, jnp.left_shift(turned, 8)),
        jnp.where(first, turned, jnp.left_shift(tile, 8)),
    ]


def key_side(keys):
    blocks = []
    for s in range(WORD_BYTES):
        for p in range(len(keys[0])):
            for h in range(DIGIT_BYTES):
                tiles = [byte_of(digit_keys[p][h], s) for digit_keys in keys]
                blocks.append(jnp.concatenate(tiles, axis=1))
    return jnp.concatenate(blocks, axis=0).astype(jnp.bfloat16)


def staged_product(table, count, make_side):
    width = DIGIT_BYTES * LANES
    tiles = table.shape[1] // width

    def body(*sums):
        for i in range(tiles):
            pltpu.matmul_push_rhs(
                table[:, i * width : (i + 1) * width], staging_register=i // MXUS, mxu_index=i % MXUS
            )
        side = make_side()
        for i in range(tiles):
            pltpu.matmul_acc_lhs(sums[i], side, load_staged_rhs=i // MXUS)
        parts = [pltpu.matmul_pop(one) for one in sums]
        return jnp.concatenate(parts, axis=1).astype(jnp.int32)

    return pl.run_scoped(
        body, *(pltpu.ACC(i % MXUS)((count, width), jnp.float32) for i in range(tiles))
    )


def switch(toeplitz, make_keys, rows):
    products = staged_product(
        toeplitz, WORD_BYTES * 2 * DIGIT_BYTES * rows, lambda: key_side(make_keys())
    )
    lane = iota((rows, LANES), 1)
    sums = []
    for p in range(2):
        total = jnp.zeros((rows, LANES), jnp.int32)
        for h in range(DIGIT_BYTES):
            words = None
            for s in range(WORD_BYTES):
                at = ((s * 2 + p) * DIGIT_BYTES + h) * rows
                term = jnp.left_shift(products[at : at + rows], 8 * s)
                words = term if words is None else words + term
            out = words[:, :LANES]
            for q in range(1, rows):
                out = out + shifted(words[:, q * LANES : (q + 1) * LANES], q * LANES)
            if h:
                turn = h * SPAN
                carried = pltpu.roll(shifted(out, LANES), turn, 1)
                out = jnp.where(lane >= turn, pltpu.roll(out, turn, 1), carried)
            total = total + out
        sums.append(total)
    return sums


def switch_tail(table, make_words, rows):
    def side():
        words = make_words()
        moved = [jnp.left_shift(words, 8 * a) for a in range(DIGIT_BYTES)]
        return jnp.concatenate(
            [
                jnp.concatenate([byte_of(part, s) for part in moved], axis=1)
                for s in range(WORD_BYTES)
            ],
            axis=0,
        ).astype(jnp.bfloat16)

    products = staged_product(table, WORD_BYTES * rows, side)
    total = products[:rows]
    for s in range(1, WORD_BYTES):
        total = total + jnp.left_shift(products[s * rows : (s + 1) * rows], 8 * s)
    out = total[:, :LANES]
    for q in range(1, rows):
        out = out + shifted(total[:, q * LANES : (q + 1) * LANES], q * LANES)
    return out


def fold_tiles(tiles):
    line = iota(tiles[0].shape, 0)
    apart = len(tiles) // 2
    while apart:
        low = jnp.bitwise_and(line, apart) == 0
        folded = []
        for first, second in zip(tiles[:apart], tiles[apart:]):
            kept = jnp.where(low, first, second)
            other = jnp.where(low, second, first)
            down = pltpu.roll(other, apart, 0)
            if 2 * apart < line.shape[0]:
                down = jnp.where(low, pltpu.roll(other, line.shape[0] - apart, 0), down)
            folded.append(kept + down)
        tiles = folded
        apart //= 2
    return tiles[0]


def kernel(
    n, slots, share, width, assign_hbm, database_hbm, queries_hbm, keys_hbm, hint_hbm, out,
    assign, query_scalars, database, keys, hint, loaded, unit_part, unit_keys, masks,
    ans_send, key_send, ans_recv, key_recv, key_words, toeplitz, tail, held,
    ready, ans_got, key_got,
):
    me = lax.axis_index("col")
    clients, columns = query_scalars.shape
    polys, cycle = hint.shape
    rows = cycle // LANES
    key_rows = key_send.shape[1] // slots
    key_pitch = unit_keys.shape[1]
    unit_key_rows = unit_keys.reshape(clients * polys * key_pitch, LANES)
    pieces = max(1, 4 // polys)
    piece = cycle // pieces
    size = 2
    planes = n // size
    few = n <= LANES // 8
    level_blocks = n // LEVELS
    chip = lax.div(me, size)
    partner = me + 1 - 2 * lax.rem(me, size)
    height = planes // width
    across = lax.rem(chip, width)
    along = lax.div(chip, width)
    poly_blocks = n // (LEVELS * DIGITS * 2)
    kind_held = jnp.where(me >= n - poly_blocks, LEVELS, lax.div(me, level_blocks))

    def each(count, body, start=0):
        lax.fori_loop(start, count, lambda i, c: (body(i), c)[1], 0, unroll=few)
    loads = [
        pltpu.make_async_copy(source, target, loaded.at[i // 3])
        for i, (source, target) in enumerate(
            (
                (assign_hbm, assign),
                (queries_hbm, query_scalars),
                (keys_hbm, keys),
                (hint_hbm, hint),
            )
        )
    ]
    for load in loads[:3]:
        load.start()
    for p in range(polys):
        for j in range(pieces):
            at = pl.ds(j * piece, piece)
            pltpu.make_async_copy(
                database_hbm.at[:, pl.ds(p * cycle + j * piece, piece)], database.at[p, :, at], loaded.at[1]
            ).start()
    for load in loads[3:]:
        load.start()
    def span(start, stop, body):
        lax.fori_loop(start, stop, lambda i, c: (body(i), c)[1], 0)

    def on_chips(start, stop, column, body):
        def both(i):
            first = (i * width + column) * size
            for core in range(size):
                body(first + core)

        span(start, stop, both)

    sent = loaded.at[0]
    barrier = pltpu.get_barrier_semaphore()

    def greet(there):
        pl.semaphore_signal(barrier, inc=1, device_id={"col": there})

    greet(partner)
    for column in range(width):
        on_chips(
            jnp.where(column < across, height, along + jnp.where(column == across, 1, 0)),
            height,
            column,
            greet,
        )
    pl.semaphore_wait(barrier, (along + 1) * (across + 1) * size - 1)

    def announce(stage, chips):
        @pl.when(chip == chips - 1)
        def _():
            def tell(i):
                there = i * size + lax.rem(me, size)
                pl.semaphore_signal(ready.at[stage], inc=1, device_id={"col": there})

            span(0, chips - 1, tell)

    announce(0, planes // 2)
    announce(1, planes)
    for load in loads[:3]:
        load.wait()
    lane_owner = iota((clients, LANES), 1) // (LANES // share)
    for j in range(key_rows):
        tile = keys[:, j * LANES : (j + 1) * LANES]
        if share > 1:
            tile = jnp.where(lane_owner == lax.rem(me, share), tile, 0)
        for p in range(polys):
            unit_key_rows[pl.ds(p * key_pitch + j, clients, stride=polys * key_pitch), :] = tile

    def stage_keys(owner):
        for k in range(slots):
            key_send[owner, k * key_rows : (k + 1) * key_rows, :] = unit_keys[assign[owner * slots + k]][:key_rows]

    def stage_answers(owner):
        for k in range(slots):
            ans_send[owner, k * rows : (k + 1) * rows, :] = unit_part[assign[owner * slots + k]]

    def send_keys(there):
        pltpu.make_async_remote_copy(
            src_ref=key_send.at[there],
            dst_ref=key_recv.at[me],
            send_sem=sent,
            recv_sem=key_got.at[kind_held],
            device_id={"col": there},
        ).start()

    def send_answers(there):
        pltpu.make_async_remote_copy(
            src_ref=ans_send.at[there],
            dst_ref=ans_recv.at[me],
            send_sem=sent,
            recv_sem=ans_got,
            device_id={"col": there},
        ).start()

    def to_first(send):
        @pl.when(chip > 0)
        def _():
            for core in range(size):
                send(core)

    def to_early(send):
        for column in range(width):
            on_chips(
                0 if column else 1,
                jnp.where(column > across, 0, along + jnp.where(column == across, 0, 1)),
                column,
                send,
            )
        send(partner)

    def to_late(stage, send):
        for column in range(width):
            start = jnp.where(column > across, 0, along + 1)
            if stage:
                start = jnp.maximum(start, jnp.where(along < height // 2, height // 2, 0))
            on_chips(start, height // 2 if stage == 0 else height, column, send)
    for core in range(size):
        stage_keys(core)
    to_first(send_keys)
    each(n, stage_keys, size)
    pltpu.make_async_copy(key_send.at[me], key_recv.at[me], key_got.at[kind_held]).start()

    line = iota((columns, LANES), 0)

    def query_column(client):
        column = jnp.zeros((columns, LANES), jnp.int32)
        for j in range(columns):
            column = jnp.where(line == j, query_scalars[client, j], column)
        return column

    def answer(poly, column):
        bytes_held = database[poly]
        tiles = []
        for q in range(rows):
            terms = bytes_held[:, q * LANES : (q + 1) * LANES] * column
            tile = terms[:rows]
            for j in range(rows, columns, rows):
                tile = tile + terms[j : j + rows]
            tiles.append(tile)
        return fold_tiles(tiles)

    first_units = [assign[core * slots + k] for core in range(size) for k in range(slots)]
    first_queries = [query_column(lax.div(unit, polys)) for unit in first_units]
    pltpu.make_async_copy(database, database, loaded.at[1]).wait()
    loads[3].wait()
    for i, (unit, column) in enumerate(zip(first_units, first_queries)):
        core, k = divmod(i, slots)
        ans_send[core, k * rows : (k + 1) * rows, :] = answer(lax.rem(unit, polys), column)
    to_first(send_answers)
    to_early(send_keys)

    def client_answers(client):
        column = query_column(client)

        def poly_answer(poly):
            unit_part[client * polys + poly] = answer(poly, column)

        each(polys, poly_answer)

    each(clients, client_answers)
    each(n, stage_answers, size)
    to_early(send_answers)
    pltpu.make_async_copy(ans_send.at[me], ans_recv.at[me], ans_got).start()
    for p in range(polys):
        for q in range(rows):
            masks[p, q : q + 1, :] = hint[p : p + 1, q * LANES : (q + 1) * LANES]

    def first_mask(k):
        return masks[lax.rem(assign[me * slots + k], polys)]

    fill_toeplitz(automorph(first_mask(0), 0), toeplitz)
    def when_ready(stage, chips):
        @pl.when((along < chips // width) & (chip != chips - 1))
        def _():
            pl.semaphore_wait(ready.at[stage], 1)
            to_late(stage, send_keys)
            to_late(stage, send_answers)

    when_ready(0, planes // 2)

    when_ready(1, planes)

    def wait_blocks(buffer, semaphore, start, count):
        blocks = buffer.at[pl.ds(start, count)]
        pltpu.make_async_copy(blocks, blocks, semaphore).wait()
    switched = []

    def gather_keys(k, kind, start, stop):
        if k == 0:
            wait_blocks(key_recv, key_got.at[kind], start, stop - start)
        for j in range(start // share, stop // share):
            block = key_recv[j * share, k * key_rows : (k + 1) * key_rows, :]
            for i in range(1, share):
                block = block + key_recv[j * share + i, k * key_rows : (k + 1) * key_rows, :]
            key_words[j * key_rows : (j + 1) * key_rows, :] = block

    def key_poly(level, t, p):
        at = ((level * DIGITS + t) * 2 + p) * rows
        return key_words[at : at + rows, :]

    def key_polys(level):
        return [[spread(key_poly(level, t, p)) for p in range(2)] for t in range(DIGITS)]

    last = LEVELS - 1
    for k in range(slots):
        mask = first_mask(k)
        if k:
            fill_toeplitz(automorph(mask, 0), toeplitz)
        added = []
        for level in range(last):

            def make_keys():
                gather_keys(k, level, level * level_blocks, (level + 1) * level_blocks)
                return key_polys(level)

            to_mask, to_value = switch(toeplitz, make_keys, rows)
            mask = mask + to_mask
            added.append(to_value)
            turned = automorph(mask, level + 1)
            fill_toeplitz(turned, toeplitz)
        early, late = n - level_blocks, n - poly_blocks
        @pl.when(chip > 0)
        def _():
            def make_keys():
                gather_keys(k, last, early, late)
                gather_keys(k, LEVELS, late, n)
                return key_polys(last)

            to_mask, to_value = switch(toeplitz, make_keys, rows)
            held[k, 0] = mask + to_mask
            held[k, 1] = to_value

        @pl.when(chip == 0)
        def _():
            def make_keys():
                gather_keys(k, last, early, late)
                polys_held = key_polys(last)
                polys_held[-1][-1] = [jnp.zeros((rows, LANES), jnp.int32)] * DIGIT_BYTES
                return polys_held

            to_mask, to_value = switch(toeplitz, make_keys, rows)
            held[k, 0] = mask + to_mask
            fill_tail(turned, tail)

            def tail_words():
                gather_keys(k, LEVELS, late, n)
                return key_poly(last, DIGITS - 1, 1)

            held[k, 1] = to_value + switch_tail(tail, tail_words, rows)

        switched.append(added)
    wait_blocks(ans_recv, ans_got, 0, n)
    for k, added in enumerate(switched):
        mask = held[k, 0]
        added = added + [held[k, 1]]
        value = ans_recv[0, k * rows : (k + 1) * rows, :]
        for j in range(1, n):
            value = value + ans_recv[j, k * rows : (k + 1) * rows, :]
        for level in range(LEVELS):
            value = value + automorph(value, level) + added[level]
        for index, words in enumerate((mask, value)):
            scaled = words.astype(jnp.float32) * 2.0 ** (-32)
            for q in range(rows):
                out[k, index : index + 1, q * LANES : (q + 1) * LANES] = scaled[q : q + 1]
    wait_blocks(key_send, sent, 0, n - 1)
    wait_blocks(ans_send, sent, 0, n - 1)


def solution(mesh):
    n = mesh.shape["col"]
    across = 2

    def on_device(database, queries, key_rows, hint, assignment):
        clients = queries.shape[0]
        polys, cycle = hint.shape
        rows = cycle // LANES
        slots = assignment.shape[0] // n
        width = key_rows.shape[1]
        share = max(1, LANES // width)
        if share > 1:
            key_rows = jnp.tile(key_rows, (1, share))
        tiles = key_rows.shape[1] // LANES
        place = pl.BlockSpec(memory_space=pltpu.HBM)
        return pl.pallas_call(
            functools.partial(kernel, n, slots, share, across),
            out_shape=pltpu.VMEM((slots, 2, cycle), jnp.float32),
            in_specs=[place] * 5,
            out_specs=pl.BlockSpec(memory_space=pltpu.VMEM),
            scratch_shapes=[
                pltpu.SMEM(assignment.shape, jnp.int32),
                pltpu.SMEM(queries.shape, jnp.int32),
                pltpu.VMEM((polys, database.shape[0], cycle), jnp.int32),
                pltpu.VMEM(key_rows.shape, jnp.int32),
                pltpu.VMEM(hint.shape, jnp.int32),
                pltpu.SemaphoreType.DMA((2,)),
                pltpu.VMEM((polys * clients, rows, LANES), jnp.int32),
                pltpu.VMEM((polys * clients, -(-tiles // 8) * 8, LANES), jnp.int32),
                pltpu.VMEM((polys, rows, LANES), jnp.int32),
                pltpu.VMEM((n, slots * rows, LANES), jnp.int32),
                pltpu.VMEM((n, slots * tiles, LANES), jnp.int32),
                pltpu.VMEM((n, slots * rows, LANES), jnp.int32),
                pltpu.VMEM((n, slots * tiles, LANES), jnp.int32),
                pltpu.VMEM((n // share * tiles, LANES), jnp.int32),
                pltpu.VMEM((WORD_BYTES * SPAN, cycle), jnp.bfloat16),
                pltpu.VMEM((DIGIT_BYTES * LANES, cycle), jnp.bfloat16),
                pltpu.VMEM((slots, 2, rows, LANES), jnp.int32),
                pltpu.SemaphoreType.REGULAR((2,)),
                pltpu.SemaphoreType.DMA,
                pltpu.SemaphoreType.DMA((LEVELS + 1,)),
            ],
            compiler_params=pltpu.CompilerParams(
                collective_id=0, has_side_effects=True
            ),
        )(*(pltpu.with_memory_space_constraint(x, pltpu.HBM) for x in (assignment, database, queries, key_rows, hint)))

    placed = (P("col", "grp"), P("grp", "col"), P("grp", "col"), P("grp", None), P("grp"))
    return jax.shard_map(
        on_device,
        mesh=mesh,
        in_specs=placed,
        out_specs=P(("grp", "col"), None, None),
        check_vma=False,
    )
```

```python
import functools

import jax
import jax.numpy as jnp
from jax import lax
from jax.experimental import pallas as pl
from jax.experimental.pallas import tpu as pltpu
from jax.sharding import PartitionSpec as P

LEVELS = 2
DIGITS = 2
LANES = 128
WORD_BYTES = 4
DIGIT_BYTES = WORD_BYTES // DIGITS
SPAN = LANES // DIGIT_BYTES
MXUS = 2


def iota(shape, axis):
    return lax.broadcasted_iota(jnp.int32, shape, axis)


def byte_of(words, index):
    return jnp.bitwise_and(jnp.right_shift(words, 8 * index), 255).astype(jnp.float32)


def shifted(poly, amount):
    rows = poly.shape[0]
    amount = amount % (2 * rows * LANES)
    negate, turn = divmod(amount // LANES, rows)
    moved = poly
    if turn:
        moved = pltpu.roll(poly, turn, 0)
        moved = jnp.where(iota(poly.shape, 0) >= turn, moved, -moved)
    return -moved if negate else moved


def automorph(poly, level):
    step = poly.shape[0] * LANES >> level
    period = 2 << level
    residue = jnp.bitwise_and(iota(poly.shape, 1), period - 1)
    out = poly
    for m in range(1, period):
        out = jnp.where(residue == m, shifted(poly, step * m), out)
    return out


def fill_rows(word_poly, table, offset, placed):
    rows = word_poly.shape[0]
    block = (SPAN, LANES)
    ahead = iota(block, 1) >= iota(block, 0) + offset

    def turned(q):
        row = jnp.broadcast_to(word_poly[q : q + 1], block)
        return pltpu.roll(row, offset, 1, stride=1, stride_axis=0)

    before = turned(rows - 1)
    for q in range(rows):
        here = turned(q)
        words = jnp.where(ahead, here, before)
        for b, at in placed:
            part = byte_of(words, b)
            if q == 0:
                part = jnp.where(ahead, part, -part)
            table[at : at + SPAN, q * LANES : (q + 1) * LANES] = part.astype(jnp.bfloat16)
        before = here


def fill_toeplitz(word_poly, toeplitz):
    fill_rows(word_poly, toeplitz, 0, [(b, b * SPAN) for b in range(WORD_BYTES)])


def fill_tail(word_poly, table):
    for offset in range(0, LANES, SPAN):
        fill_rows(
            word_poly,
            table,
            offset,
            [((DIGITS - 1) * DIGIT_BYTES + a, a * LANES + offset) for a in range(DIGIT_BYTES)],
        )


def spread(tile):
    first = iota(tile.shape, 1) < SPAN
    turned = pltpu.roll(tile, SPAN, 1)
    return [
        jnp.where(first, tile, jnp.left_shift(turned, 8)),
        jnp.where(first, turned, jnp.left_shift(tile, 8)),
    ]


def key_side(keys):
    blocks = []
    for s in range(WORD_BYTES):
        for p in range(len(keys[0])):
            for h in range(DIGIT_BYTES):
                tiles = [byte_of(digit_keys[p][h], s) for digit_keys in keys]
                blocks.append(jnp.concatenate(tiles, axis=1))
    return jnp.concatenate(blocks, axis=0).astype(jnp.bfloat16)


def staged_product(table, count, make_side):
    width = DIGIT_BYTES * LANES
    tiles = table.shape[1] // width

    def body(*sums):
        for i in range(tiles):
            pltpu.matmul_push_rhs(
                table[:, i * width : (i + 1) * width], staging_register=i // MXUS, mxu_index=i % MXUS
            )
        side = make_side()
        for i in range(tiles):
            pltpu.matmul_acc_lhs(sums[i], side, load_staged_rhs=i // MXUS)
        parts = [pltpu.matmul_pop(one) for one in sums]
        return jnp.concatenate(parts, axis=1).astype(jnp.int32)

    return pl.run_scoped(
        body, *(pltpu.ACC(i % MXUS)((count, width), jnp.float32) for i in range(tiles))
    )


def switch(toeplitz, make_keys, rows):
    products = staged_product(
        toeplitz, WORD_BYTES * 2 * DIGIT_BYTES * rows, lambda: key_side(make_keys())
    )
    lane = iota((rows, LANES), 1)
    sums = []
    for p in range(2):
        total = jnp.zeros((rows, LANES), jnp.int32)
        for h in range(DIGIT_BYTES):
            words = None
            for s in range(WORD_BYTES):
                at = ((s * 2 + p) * DIGIT_BYTES + h) * rows
                term = jnp.left_shift(products[at : at + rows], 8 * s)
                words = term if words is None else words + term
            out = words[:, :LANES]
            for q in range(1, rows):
                out = out + shifted(words[:, q * LANES : (q + 1) * LANES], q * LANES)
            if h:
                turn = h * SPAN
                carried = pltpu.roll(shifted(out, LANES), turn, 1)
                out = jnp.where(lane >= turn, pltpu.roll(out, turn, 1), carried)
            total = total + out
        sums.append(total)
    return sums


def switch_tail(table, make_words, rows):
    def side():
        words = make_words()
        moved = [jnp.left_shift(words, 8 * a) for a in range(DIGIT_BYTES)]
        return jnp.concatenate(
            [
                jnp.concatenate([byte_of(part, s) for part in moved], axis=1)
                for s in range(WORD_BYTES)
            ],
            axis=0,
        ).astype(jnp.bfloat16)

    products = staged_product(table, WORD_BYTES * rows, side)
    total = products[:rows]
    for s in range(1, WORD_BYTES):
        total = total + jnp.left_shift(products[s * rows : (s + 1) * rows], 8 * s)
    out = total[:, :LANES]
    for q in range(1, rows):
        out = out + shifted(total[:, q * LANES : (q + 1) * LANES], q * LANES)
    return out


def fold_tiles(tiles):
    line = iota(tiles[0].shape, 0)
    apart = len(tiles) // 2
    while apart:
        low = jnp.bitwise_and(line, apart) == 0
        folded = []
        for first, second in zip(tiles[:apart], tiles[apart:]):
            kept = jnp.where(low, first, second)
            other = jnp.where(low, second, first)
            down = pltpu.roll(other, apart, 0)
            if 2 * apart < line.shape[0]:
                down = jnp.where(low, pltpu.roll(other, line.shape[0] - apart, 0), down)
            folded.append(kept + down)
        tiles = folded
        apart //= 2
    return tiles[0]


def kernel(*refs):
    pl.run_scoped(functools.partial(scoped, *refs), pltpu.SemaphoreType.DMA((2,)))


def scoped(
    n, slots, share, width, assign_hbm, database_hbm, queries_hbm, keys_hbm, hint_hbm, out,
    assign, query_scalars, database, keys, hint, unit_part, unit_keys, masks,
    ans_send, key_send, ans_recv, key_recv, key_words, toeplitz, tail, held,
    ready, ans_got, key_got, loaded,
):
    me = lax.axis_index("col")
    clients, columns = query_scalars.shape
    polys, cycle = hint.shape
    rows = cycle // LANES
    key_rows = key_send.shape[1] // slots
    key_pitch = unit_keys.shape[1]
    unit_key_rows = unit_keys.reshape(clients * polys * key_pitch, LANES)
    pieces = max(1, 4 // polys)
    piece = cycle // pieces
    size = 2
    planes = n // size
    few = n <= LANES // 8
    level_blocks = n // LEVELS
    chip = lax.div(me, size)
    partner = me + 1 - 2 * lax.rem(me, size)
    height = planes // width
    across = lax.rem(chip, width)
    along = lax.div(chip, width)
    poly_blocks = n // (LEVELS * DIGITS * 2)
    kind_held = jnp.where(me >= n - poly_blocks, LEVELS, lax.div(me, level_blocks))

    def each(count, body, start=0):
        lax.fori_loop(start, count, lambda i, c: (body(i), c)[1], 0, unroll=few)
    loads = [
        pltpu.make_async_copy(source, target, loaded.at[i // 3])
        for i, (source, target) in enumerate(
            (
                (assign_hbm, assign),
                (queries_hbm, query_scalars),
                (keys_hbm, keys),
                (hint_hbm, hint),
            )
        )
    ]
    for load in loads[:3]:
        load.start()
    for p in range(polys):
        for j in range(pieces):
            at = pl.ds(j * piece, piece)
            pltpu.make_async_copy(
                database_hbm.at[:, pl.ds(p * cycle + j * piece, piece)], database.at[p, :, at], loaded.at[1]
            ).start()
    for load in loads[3:]:
        load.start()
    def span(start, stop, body):
        lax.fori_loop(start, stop, lambda i, c: (body(i), c)[1], 0)

    def on_chips(start, stop, column, body):
        def both(i):
            first = (i * width + column) * size
            for core in range(size):
                body(first + core)

        span(start, stop, both)

    sent = loaded.at[0]
    barrier = pltpu.get_barrier_semaphore()

    def greet(there):
        pl.semaphore_signal(barrier, inc=1, device_id={"col": there})

    greet(partner)
    for column in range(width):
        on_chips(
            jnp.where(column < across, height, along + jnp.where(column == across, 1, 0)),
            height,
            column,
            greet,
        )
    pl.semaphore_wait(barrier, (along + 1) * (across + 1) * size - 1)

    def announce(stage, chips):
        @pl.when(chip == chips - 1)
        def _():
            def tell(i):
                there = i * size + lax.rem(me, size)
                pl.semaphore_signal(ready.at[stage], inc=1, device_id={"col": there})

            span(0, chips - 1, tell)

    announce(0, planes // 2)
    announce(1, planes)
    for load in loads[:3]:
        load.wait()
    lane_owner = iota((clients, LANES), 1) // (LANES // share)
    for j in range(key_rows):
        tile = keys[:, j * LANES : (j + 1) * LANES]
        if share > 1:
            tile = jnp.where(lane_owner == lax.rem(me, share), tile, 0)
        for p in range(polys):
            unit_key_rows[pl.ds(p * key_pitch + j, clients, stride=polys * key_pitch), :] = tile

    def stage_keys(owner):
        for k in range(slots):
            key_send[owner, k * key_rows : (k + 1) * key_rows, :] = unit_keys[assign[owner * slots + k]][:key_rows]

    def stage_answers(owner):
        for k in range(slots):
            ans_send[owner, k * rows : (k + 1) * rows, :] = unit_part[assign[owner * slots + k]]

    def send_keys(there):
        pltpu.make_async_remote_copy(
            src_ref=key_send.at[there],
            dst_ref=key_recv.at[me],
            send_sem=sent,
            recv_sem=key_got.at[kind_held],
            device_id={"col": there},
        ).start()

    def send_answers(there):
        pltpu.make_async_remote_copy(
            src_ref=ans_send.at[there],
            dst_ref=ans_recv.at[me],
            send_sem=sent,
            recv_sem=ans_got,
            device_id={"col": there},
        ).start()

    def to_first(send):
        @pl.when(chip > 0)
        def _():
            for core in range(size):
                send(core)

    def to_early(send):
        for column in range(width):
            on_chips(
                0 if column else 1,
                jnp.where(column > across, 0, along + jnp.where(column == across, 0, 1)),
                column,
                send,
            )
        send(partner)

    def to_late(stage, send):
        for column in range(width):
            start = jnp.where(column > across, 0, along + 1)
            if stage:
                start = jnp.maximum(start, jnp.where(along < height // 2, height // 2, 0))
            on_chips(start, height // 2 if stage == 0 else height, column, send)
    each(n, stage_keys)
    to_first(send_keys)
    pltpu.make_async_copy(key_send.at[me], key_recv.at[me], key_got.at[kind_held]).start()

    line = iota((columns, LANES), 0)

    def query_column(client):
        column = jnp.zeros((columns, LANES), jnp.int32)
        for j in range(columns):
            column = jnp.where(line == j, query_scalars[client, j], column)
        return column

    def answer(poly, column):
        bytes_held = database[poly]
        tiles = []
        for q in range(rows):
            terms = bytes_held[:, q * LANES : (q + 1) * LANES] * column
            tile = terms[:rows]
            for j in range(rows, columns, rows):
                tile = tile + terms[j : j + rows]
            tiles.append(tile)
        return fold_tiles(tiles)

    first_units = [assign[core * slots + k] for core in range(size) for k in range(slots)]
    first_queries = [query_column(lax.div(unit, polys)) for unit in first_units]
    pltpu.make_async_copy(database, database, loaded.at[1]).wait()
    loads[3].wait()
    for i, (unit, column) in enumerate(zip(first_units, first_queries)):
        core, k = divmod(i, slots)
        ans_send[core, k * rows : (k + 1) * rows, :] = answer(lax.rem(unit, polys), column)
    to_first(send_answers)
    to_early(send_keys)

    def client_answers(client):
        column = query_column(client)

        def poly_answer(poly):
            unit_part[client * polys + poly] = answer(poly, column)

        each(polys, poly_answer)

    each(clients, client_answers)
    each(n, stage_answers, size)
    to_early(send_answers)
    pltpu.make_async_copy(ans_send.at[me], ans_recv.at[me], ans_got).start()
    for p in range(polys):
        for q in range(rows):
            masks[p, q : q + 1, :] = hint[p : p + 1, q * LANES : (q + 1) * LANES]

    def first_mask(k):
        return masks[lax.rem(assign[me * slots + k], polys)]

    fill_toeplitz(automorph(first_mask(0), 0), toeplitz)
    def when_ready(stage, chips):
        @pl.when((along < chips // width) & (chip != chips - 1))
        def _():
            pl.semaphore_wait(ready.at[stage], 1)
            to_late(stage, send_keys)
            to_late(stage, send_answers)

    when_ready(0, planes // 2)

    when_ready(1, planes)

    def wait_blocks(buffer, semaphore, start, count):
        blocks = buffer.at[pl.ds(start, count)]
        pltpu.make_async_copy(blocks, blocks, semaphore).wait()
    switched = []

    def gather_keys(k, kind, start, stop):
        if k == 0:
            wait_blocks(key_recv, key_got.at[kind], start, stop - start)
        for j in range(start // share, stop // share):
            block = key_recv[j * share, k * key_rows : (k + 1) * key_rows, :]
            for i in range(1, share):
                block = block + key_recv[j * share + i, k * key_rows : (k + 1) * key_rows, :]
            key_words[j * key_rows : (j + 1) * key_rows, :] = block

    def key_poly(level, t, p):
        at = ((level * DIGITS + t) * 2 + p) * rows
        return key_words[at : at + rows, :]

    def key_polys(level):
        return [[spread(key_poly(level, t, p)) for p in range(2)] for t in range(DIGITS)]

    last = LEVELS - 1
    for k in range(slots):
        mask = first_mask(k)
        if k:
            fill_toeplitz(automorph(mask, 0), toeplitz)
        added = []
        for level in range(last):

            def make_keys():
                gather_keys(k, level, level * level_blocks, (level + 1) * level_blocks)
                return key_polys(level)

            to_mask, to_value = switch(toeplitz, make_keys, rows)
            mask = mask + to_mask
            added.append(to_value)
            turned = automorph(mask, level + 1)
            fill_toeplitz(turned, toeplitz)
        early, late = n - level_blocks, n - poly_blocks
        @pl.when(chip > 0)
        def _():
            def make_keys():
                gather_keys(k, last, early, late)
                gather_keys(k, LEVELS, late, n)
                return key_polys(last)

            to_mask, to_value = switch(toeplitz, make_keys, rows)
            held[k, 0] = mask + to_mask
            held[k, 1] = to_value

        @pl.when(chip == 0)
        def _():
            def make_keys():
                gather_keys(k, last, early, late)
                polys_held = key_polys(last)
                polys_held[-1][-1] = [jnp.zeros((rows, LANES), jnp.int32)] * DIGIT_BYTES
                return polys_held

            to_mask, to_value = switch(toeplitz, make_keys, rows)
            held[k, 0] = mask + to_mask
            fill_tail(turned, tail)

            def tail_words():
                gather_keys(k, LEVELS, late, n)
                return key_poly(last, DIGITS - 1, 1)

            held[k, 1] = to_value + switch_tail(tail, tail_words, rows)

        switched.append(added)

    def write(k, index, words):
        scaled = words.astype(jnp.float32) * 2.0 ** (-32)
        for q in range(rows):
            out[k, index : index + 1, q * LANES : (q + 1) * LANES] = scaled[q : q + 1]

    for k in range(slots):
        write(k, 0, held[k, 0])
    wait_blocks(ans_recv, ans_got, 0, n)
    for k, added in enumerate(switched):
        added = added + [held[k, 1]]
        value = ans_recv[0, k * rows : (k + 1) * rows, :]
        for j in range(1, n):
            value = value + ans_recv[j, k * rows : (k + 1) * rows, :]
        for level in range(LEVELS):
            value = value + automorph(value, level) + added[level]
        write(k, 1, value)
    wait_blocks(key_send, sent, 0, n - 1)
    wait_blocks(ans_send, sent, 0, n - 1)


def solution(mesh):
    n = mesh.shape["col"]
    across = 2

    def on_device(database, queries, key_rows, hint, assignment):
        clients = queries.shape[0]
        polys, cycle = hint.shape
        rows = cycle // LANES
        slots = assignment.shape[0] // n
        width = key_rows.shape[1]
        share = max(1, LANES // width)
        if share > 1:
            key_rows = jnp.tile(key_rows, (1, share))
        tiles = key_rows.shape[1] // LANES
        place = pl.BlockSpec(memory_space=pltpu.HBM)
        return pl.pallas_call(
            functools.partial(kernel, n, slots, share, across),
            out_shape=pltpu.VMEM((slots, 2, cycle), jnp.float32),
            in_specs=[place] * 5,
            out_specs=pl.BlockSpec(memory_space=pltpu.VMEM),
            scratch_shapes=[
                pltpu.SMEM(assignment.shape, jnp.int32),
                pltpu.SMEM(queries.shape, jnp.int32),
                pltpu.VMEM((polys, database.shape[0], cycle), jnp.int32),
                pltpu.VMEM(key_rows.shape, jnp.int32),
                pltpu.VMEM(hint.shape, jnp.int32),
                pltpu.VMEM((polys * clients, rows, LANES), jnp.int32),
                pltpu.VMEM((polys * clients, -(-tiles // 8) * 8, LANES), jnp.int32),
                pltpu.VMEM((polys, rows, LANES), jnp.int32),
                pltpu.VMEM((n, slots * rows, LANES), jnp.int32),
                pltpu.VMEM((n, slots * tiles, LANES), jnp.int32),
                pltpu.VMEM((n, slots * rows, LANES), jnp.int32),
                pltpu.VMEM((n, slots * tiles, LANES), jnp.int32),
                pltpu.VMEM((n // share * tiles, LANES), jnp.int32),
                pltpu.VMEM((WORD_BYTES * SPAN, cycle), jnp.bfloat16),
                pltpu.VMEM((DIGIT_BYTES * LANES, cycle), jnp.bfloat16),
                pltpu.VMEM((slots, 2, rows, LANES), jnp.int32),
                pltpu.SemaphoreType.REGULAR((2,)),
                pltpu.SemaphoreType.DMA,
                pltpu.SemaphoreType.DMA((LEVELS + 1,)),
            ],
            compiler_params=pltpu.CompilerParams(
                collective_id=0, has_side_effects=True
            ),
        )(*(pltpu.with_memory_space_constraint(x, pltpu.HBM) for x in (assignment, database, queries, key_rows, hint)))

    placed = (P("col", "grp"), P("grp", "col"), P("grp", "col"), P("grp", None), P("grp"))
    return jax.shard_map(
        on_device,
        mesh=mesh,
        in_specs=placed,
        out_specs=P(("grp", "col"), None, None),
        check_vma=False,
    )
```

```python
import functools

import jax
import jax.numpy as jnp
from jax import lax
from jax.experimental import pallas as pl
from jax.experimental.pallas import tpu as pltpu
from jax.sharding import PartitionSpec as P

LEVELS = 2
DIGITS = 2
LANES = 128
WORD_BYTES = 4
DIGIT_BYTES = WORD_BYTES // DIGITS
SPAN = LANES // DIGIT_BYTES
MXUS = 2


def iota(shape, axis):
    return lax.broadcasted_iota(jnp.int32, shape, axis)


def byte_of(words, index):
    return jnp.bitwise_and(jnp.right_shift(words, 8 * index), 255).astype(jnp.float32)


def shifted(poly, amount):
    rows = poly.shape[0]
    amount = amount % (2 * rows * LANES)
    negate, turn = divmod(amount // LANES, rows)
    moved = poly
    if turn:
        moved = pltpu.roll(poly, turn, 0)
        moved = jnp.where(iota(poly.shape, 0) >= turn, moved, -moved)
    return -moved if negate else moved


def automorph(poly, level):
    step = poly.shape[0] * LANES >> level
    period = 2 << level
    residue = jnp.bitwise_and(iota(poly.shape, 1), period - 1)
    out = poly
    for m in range(1, period):
        out = jnp.where(residue == m, shifted(poly, step * m), out)
    return out


def fill_rows(word_poly, table, offset, placed):
    rows = word_poly.shape[0]
    block = (SPAN, LANES)
    ahead = iota(block, 1) >= iota(block, 0) + offset

    def turned(q):
        row = jnp.broadcast_to(word_poly[q : q + 1], block)
        return pltpu.roll(row, offset, 1, stride=1, stride_axis=0)

    before = turned(rows - 1)
    for q in range(rows):
        here = turned(q)
        words = jnp.where(ahead, here, before)
        for b, at in placed:
            part = byte_of(words, b)
            if q == 0:
                part = jnp.where(ahead, part, -part)
            table[at : at + SPAN, q * LANES : (q + 1) * LANES] = part.astype(jnp.bfloat16)
        before = here


def fill_toeplitz(word_poly, toeplitz):
    fill_rows(word_poly, toeplitz, 0, [(b, b * SPAN) for b in range(WORD_BYTES)])


def fill_tail(word_poly, table):
    for offset in range(0, LANES, SPAN):
        fill_rows(
            word_poly,
            table,
            offset,
            [((DIGITS - 1) * DIGIT_BYTES + a, a * LANES + offset) for a in range(DIGIT_BYTES)],
        )


def spread(tile):
    first = iota(tile.shape, 1) < SPAN
    turned = pltpu.roll(tile, SPAN, 1)
    return [
        jnp.where(first, tile, jnp.left_shift(turned, 8)),
        jnp.where(first, turned, jnp.left_shift(tile, 8)),
    ]


def key_side(keys):
    blocks = []
    for s in range(WORD_BYTES):
        for p in range(len(keys[0])):
            for h in range(DIGIT_BYTES):
                tiles = [byte_of(digit_keys[p][h], s) for digit_keys in keys]
                blocks.append(jnp.concatenate(tiles, axis=1))
    return jnp.concatenate(blocks, axis=0).astype(jnp.bfloat16)


def staged_product(table, count, make_side):
    width = DIGIT_BYTES * LANES
    tiles = table.shape[1] // width

    def body(*sums):
        for i in range(tiles):
            pltpu.matmul_push_rhs(
                table[:, i * width : (i + 1) * width], staging_register=i // MXUS, mxu_index=i % MXUS
            )
        side = make_side()
        for i in range(tiles):
            pltpu.matmul_acc_lhs(sums[i], side, load_staged_rhs=i // MXUS)
        parts = [pltpu.matmul_pop(one) for one in sums]
        return jnp.concatenate(parts, axis=1).astype(jnp.int32)

    return pl.run_scoped(
        body, *(pltpu.ACC(i % MXUS)((count, width), jnp.float32) for i in range(tiles))
    )


def switch(toeplitz, make_keys, rows):
    products = staged_product(
        toeplitz, WORD_BYTES * 2 * DIGIT_BYTES * rows, lambda: key_side(make_keys())
    )
    lane = iota((rows, LANES), 1)
    sums = []
    for p in range(2):
        total = jnp.zeros((rows, LANES), jnp.int32)
        for h in range(DIGIT_BYTES):
            words = None
            for s in range(WORD_BYTES):
                at = ((s * 2 + p) * DIGIT_BYTES + h) * rows
                term = jnp.left_shift(products[at : at + rows], 8 * s)
                words = term if words is None else words + term
            out = words[:, :LANES]
            for q in range(1, rows):
                out = out + shifted(words[:, q * LANES : (q + 1) * LANES], q * LANES)
            if h:
                turn = h * SPAN
                carried = pltpu.roll(shifted(out, LANES), turn, 1)
                out = jnp.where(lane >= turn, pltpu.roll(out, turn, 1), carried)
            total = total + out
        sums.append(total)
    return sums


def switch_tail(table, make_words, rows):
    def side():
        words = make_words()
        moved = [jnp.left_shift(words, 8 * a) for a in range(DIGIT_BYTES)]
        return jnp.concatenate(
            [
                jnp.concatenate([byte_of(part, s) for part in moved], axis=1)
                for s in range(WORD_BYTES)
            ],
            axis=0,
        ).astype(jnp.bfloat16)

    products = staged_product(table, WORD_BYTES * rows, side)
    total = products[:rows]
    for s in range(1, WORD_BYTES):
        total = total + jnp.left_shift(products[s * rows : (s + 1) * rows], 8 * s)
    out = total[:, :LANES]
    for q in range(1, rows):
        out = out + shifted(total[:, q * LANES : (q + 1) * LANES], q * LANES)
    return out


def fold_tiles(tiles):
    line = iota(tiles[0].shape, 0)
    apart = len(tiles) // 2
    while apart:
        low = jnp.bitwise_and(line, apart) == 0
        folded = []
        for first, second in zip(tiles[:apart], tiles[apart:]):
            kept = jnp.where(low, first, second)
            other = jnp.where(low, second, first)
            down = pltpu.roll(other, apart, 0)
            if 2 * apart < line.shape[0]:
                down = jnp.where(low, pltpu.roll(other, line.shape[0] - apart, 0), down)
            folded.append(kept + down)
        tiles = folded
        apart //= 2
    return tiles[0]


def kernel(*refs):
    pl.run_scoped(functools.partial(scoped, *refs), pltpu.SemaphoreType.DMA((2,)))


def scoped(
    n, slots, share, width, assign_hbm, database_hbm, queries_hbm, keys_hbm, hint_hbm, out,
    assign, query_scalars, database, keys, hint, unit_part, unit_keys, masks,
    ans_send, key_send, ans_recv, key_recv, key_words, toeplitz, tail, held,
    ready, ans_got, key_got, loaded,
):
    me = lax.axis_index("col")
    clients, columns = query_scalars.shape
    polys, cycle = hint.shape
    rows = cycle // LANES
    key_rows = key_send.shape[1] // slots
    key_pitch = unit_keys.shape[1]
    unit_key_rows = unit_keys.reshape(clients * polys * key_pitch, LANES)
    pieces = max(1, 4 // polys)
    piece = cycle // pieces
    size = 2
    planes = n // size
    few = n <= LANES // 8
    level_blocks = n // LEVELS
    chip = lax.div(me, size)
    partner = me + 1 - 2 * lax.rem(me, size)
    height = planes // width
    across = lax.rem(chip, width)
    along = lax.div(chip, width)
    poly_blocks = n // (LEVELS * DIGITS * 2)
    kind_held = jnp.where(me >= n - poly_blocks, LEVELS, lax.div(me, level_blocks))

    def each(count, body, start=0):
        lax.fori_loop(start, count, lambda i, c: (body(i), c)[1], 0, unroll=few)
    loads = [
        pltpu.make_async_copy(source, target, loaded.at[i // 3])
        for i, (source, target) in enumerate(
            (
                (assign_hbm, assign),
                (queries_hbm, query_scalars),
                (keys_hbm, keys),
                (hint_hbm, hint),
            )
        )
    ]
    for load in loads[:3]:
        load.start()
    for p in range(polys):
        for j in range(pieces):
            at = pl.ds(j * piece, piece)
            pltpu.make_async_copy(
                database_hbm.at[:, pl.ds(p * cycle + j * piece, piece)], database.at[p, :, at], loaded.at[1]
            ).start()
    for load in loads[3:]:
        load.start()
    def span(start, stop, body):
        lax.fori_loop(start, stop, lambda i, c: (body(i), c)[1], 0)

    def on_chips(start, stop, column, body):
        def both(i):
            first = (i * width + column) * size
            for core in range(size):
                body(first + core)

        span(start, stop, both)

    sent = loaded.at[0]
    barrier = pltpu.get_barrier_semaphore()

    def greet(there):
        pl.semaphore_signal(barrier, inc=1, device_id={"col": there})

    greet(partner)
    for column in range(width):
        on_chips(
            jnp.where(column < across, height, along + jnp.where(column == across, 1, 0)),
            height,
            column,
            greet,
        )
    pl.semaphore_wait(barrier, (along + 1) * (across + 1) * size - 1)

    def announce(stage, chips):
        @pl.when(chip == chips - 1)
        def _():
            def tell(i):
                there = i * size + lax.rem(me, size)
                pl.semaphore_signal(ready.at[stage], inc=1, device_id={"col": there})

            span(0, chips - 1, tell)

    announce(0, planes // 2)
    announce(1, planes)
    for load in loads[:3]:
        load.wait()
    lane_owner = iota((clients, LANES), 1) // (LANES // share)
    for j in range(key_rows):
        tile = keys[:, j * LANES : (j + 1) * LANES]
        if share > 1:
            tile = jnp.where(lane_owner == lax.rem(me, share), tile, 0)
        for p in range(polys):
            unit_key_rows[pl.ds(p * key_pitch + j, clients, stride=polys * key_pitch), :] = tile

    def stage_keys(owner):
        for k in range(slots):
            key_send[owner, k * key_rows : (k + 1) * key_rows, :] = unit_keys[assign[owner * slots + k]][:key_rows]

    def stage_answers(owner):
        for k in range(slots):
            ans_send[owner, k * rows : (k + 1) * rows, :] = unit_part[assign[owner * slots + k]]

    def send_keys(there):
        pltpu.make_async_remote_copy(
            src_ref=key_send.at[there],
            dst_ref=key_recv.at[me],
            send_sem=sent,
            recv_sem=key_got.at[kind_held],
            device_id={"col": there},
        ).start()

    def send_answers(there):
        pltpu.make_async_remote_copy(
            src_ref=ans_send.at[there],
            dst_ref=ans_recv.at[me],
            send_sem=sent,
            recv_sem=ans_got,
            device_id={"col": there},
        ).start()

    def to_first(send):
        @pl.when(chip > 0)
        def _():
            for core in range(size):
                send(core)

    def to_early(send):
        for column in range(width):
            on_chips(
                0 if column else 1,
                jnp.where(column > across, 0, along + jnp.where(column == across, 0, 1)),
                column,
                send,
            )
        send(partner)

    def to_late(stage, send):
        for column in range(width):
            start = jnp.where(column > across, 0, along + 1)
            if stage:
                start = jnp.maximum(start, jnp.where(along < height // 2, height // 2, 0))
            on_chips(start, height // 2 if stage == 0 else height, column, send)
    each(n, stage_keys)
    to_first(send_keys)
    pltpu.make_async_copy(key_send.at[me], key_recv.at[me], key_got.at[kind_held]).start()

    line = iota((columns, LANES), 0)

    def query_column(client):
        column = jnp.zeros((columns, LANES), jnp.int32)
        for j in range(columns):
            column = jnp.where(line == j, query_scalars[client, j], column)
        return column

    def answer(poly, column):
        bytes_held = database[poly]
        tiles = []
        for q in range(rows):
            terms = bytes_held[:, q * LANES : (q + 1) * LANES] * column
            tile = terms[:rows]
            for j in range(rows, columns, rows):
                tile = tile + terms[j : j + rows]
            tiles.append(tile)
        return fold_tiles(tiles)

    first_units = [assign[core * slots + k] for core in range(size) for k in range(slots)]
    first_queries = [query_column(lax.div(unit, polys)) for unit in first_units]
    pltpu.make_async_copy(database, database, loaded.at[1]).wait()
    loads[3].wait()
    for i, (unit, column) in enumerate(zip(first_units, first_queries)):
        core, k = divmod(i, slots)
        ans_send[core, k * rows : (k + 1) * rows, :] = answer(lax.rem(unit, polys), column)
    to_first(send_answers)

    def client_answers(client):
        column = query_column(client)

        def poly_answer(poly):
            unit_part[client * polys + poly] = answer(poly, column)

        each(polys, poly_answer)

    each(clients, client_answers)
    each(n, stage_answers, size)
    to_early(send_keys)
    to_early(send_answers)
    pltpu.make_async_copy(ans_send.at[me], ans_recv.at[me], ans_got).start()
    for p in range(polys):
        for q in range(rows):
            masks[p, q : q + 1, :] = hint[p : p + 1, q * LANES : (q + 1) * LANES]

    def first_mask(k):
        return masks[lax.rem(assign[me * slots + k], polys)]

    fill_toeplitz(automorph(first_mask(0), 0), toeplitz)
    def when_ready(stage, chips):
        @pl.when((along < chips // width) & (chip != chips - 1))
        def _():
            pl.semaphore_wait(ready.at[stage], 1)
            to_late(stage, send_keys)
            to_late(stage, send_answers)

    when_ready(0, planes // 2)

    when_ready(1, planes)

    def wait_blocks(buffer, semaphore, start, count):
        blocks = buffer.at[pl.ds(start, count)]
        pltpu.make_async_copy(blocks, blocks, semaphore).wait()
    switched = []

    def gather_keys(k, kind, start, stop):
        if k == 0:
            wait_blocks(key_recv, key_got.at[kind], start, stop - start)
        for j in range(start // share, stop // share):
            block = key_recv[j * share, k * key_rows : (k + 1) * key_rows, :]
            for i in range(1, share):
                block = block + key_recv[j * share + i, k * key_rows : (k + 1) * key_rows, :]
            key_words[j * key_rows : (j + 1) * key_rows, :] = block

    def key_poly(level, t, p):
        at = ((level * DIGITS + t) * 2 + p) * rows
        return key_words[at : at + rows, :]

    def key_polys(level):
        return [[spread(key_poly(level, t, p)) for p in range(2)] for t in range(DIGITS)]

    last = LEVELS - 1
    for k in range(slots):
        mask = first_mask(k)
        if k:
            fill_toeplitz(automorph(mask, 0), toeplitz)
        added = []
        for level in range(last):

            def make_keys():
                gather_keys(k, level, level * level_blocks, (level + 1) * level_blocks)
                return key_polys(level)

            to_mask, to_value = switch(toeplitz, make_keys, rows)
            mask = mask + to_mask
            added.append(to_value)
            turned = automorph(mask, level + 1)
            fill_toeplitz(turned, toeplitz)
        early, late = n - level_blocks, n - poly_blocks
        @pl.when(chip > 0)
        def _():
            def make_keys():
                gather_keys(k, last, early, late)
                gather_keys(k, LEVELS, late, n)
                return key_polys(last)

            to_mask, to_value = switch(toeplitz, make_keys, rows)
            held[k, 0] = mask + to_mask
            held[k, 1] = to_value

        @pl.when(chip == 0)
        def _():
            def make_keys():
                gather_keys(k, last, early, late)
                polys_held = key_polys(last)
                polys_held[-1][-1] = [jnp.zeros((rows, LANES), jnp.int32)] * DIGIT_BYTES
                return polys_held

            to_mask, to_value = switch(toeplitz, make_keys, rows)
            held[k, 0] = mask + to_mask
            fill_tail(turned, tail)

            def tail_words():
                gather_keys(k, LEVELS, late, n)
                return key_poly(last, DIGITS - 1, 1)

            held[k, 1] = to_value + switch_tail(tail, tail_words, rows)

        switched.append(added)

    def write(k, index, words):
        scaled = words.astype(jnp.float32) * 2.0 ** (-32)
        for q in range(rows):
            out[k, index : index + 1, q * LANES : (q + 1) * LANES] = scaled[q : q + 1]

    for k in range(slots):
        write(k, 0, held[k, 0])
    wait_blocks(ans_recv, ans_got, 0, n)
    for k, added in enumerate(switched):
        added = added + [held[k, 1]]
        value = ans_recv[0, k * rows : (k + 1) * rows, :]
        for j in range(1, n):
            value = value + ans_recv[j, k * rows : (k + 1) * rows, :]
        for level in range(LEVELS):
            value = value + automorph(value, level) + added[level]
        write(k, 1, value)
    wait_blocks(key_send, sent, 0, n - 1)
    wait_blocks(ans_send, sent, 0, n - 1)


def solution(mesh):
    n = mesh.shape["col"]
    across = 2

    def on_device(database, queries, key_rows, hint, assignment):
        clients = queries.shape[0]
        polys, cycle = hint.shape
        rows = cycle // LANES
        slots = assignment.shape[0] // n
        width = key_rows.shape[1]
        share = max(1, LANES // width)
        if share > 1:
            key_rows = jnp.tile(key_rows, (1, share))
        tiles = key_rows.shape[1] // LANES
        place = pl.BlockSpec(memory_space=pltpu.HBM)
        return pl.pallas_call(
            functools.partial(kernel, n, slots, share, across),
            out_shape=pltpu.VMEM((slots, 2, cycle), jnp.float32),
            in_specs=[place] * 5,
            out_specs=pl.BlockSpec(memory_space=pltpu.VMEM),
            scratch_shapes=[
                pltpu.SMEM(assignment.shape, jnp.int32),
                pltpu.SMEM(queries.shape, jnp.int32),
                pltpu.VMEM((polys, database.shape[0], cycle), jnp.int32),
                pltpu.VMEM(key_rows.shape, jnp.int32),
                pltpu.VMEM(hint.shape, jnp.int32),
                pltpu.VMEM((polys * clients, rows, LANES), jnp.int32),
                pltpu.VMEM((polys * clients, -(-tiles // 8) * 8, LANES), jnp.int32),
                pltpu.VMEM((polys, rows, LANES), jnp.int32),
                pltpu.VMEM((n, slots * rows, LANES), jnp.int32),
                pltpu.VMEM((n, slots * tiles, LANES), jnp.int32),
                pltpu.VMEM((n, slots * rows, LANES), jnp.int32),
                pltpu.VMEM((n, slots * tiles, LANES), jnp.int32),
                pltpu.VMEM((n // share * tiles, LANES), jnp.int32),
                pltpu.VMEM((WORD_BYTES * SPAN, cycle), jnp.bfloat16),
                pltpu.VMEM((DIGIT_BYTES * LANES, cycle), jnp.bfloat16),
                pltpu.VMEM((slots, 2, rows, LANES), jnp.int32),
                pltpu.SemaphoreType.REGULAR((2,)),
                pltpu.SemaphoreType.DMA,
                pltpu.SemaphoreType.DMA((LEVELS + 1,)),
            ],
            compiler_params=pltpu.CompilerParams(
                collective_id=0, has_side_effects=True
            ),
        )(*(pltpu.with_memory_space_constraint(x, pltpu.HBM) for x in (assignment, database, queries, key_rows, hint)))

    placed = (P("col", "grp"), P("grp", "col"), P("grp", "col"), P("grp", None), P("grp"))
    return jax.shard_map(
        on_device,
        mesh=mesh,
        in_specs=placed,
        out_specs=P(("grp", "col"), None, None),
        check_vma=False,
    )
```
